32 devices in a mesh: group: 2 (over y), seq: 4 (over z), head: 2 (over x), sub: 2 (over core).
Axes of the slice: x: 2, y: 2, z: 4, core: 2. Of those that a mesh axis runs over, the one named last changes fastest.
Arguments:
- query_rows: bfloat16 [4096, 2048], P(('group', 'seq', 'head', 'sub')), parts along dimension 0, may hold values from -6 to 6
- key_rows: bfloat16 [4096, 2048], P(('group', 'seq', 'head', 'sub')), parts along dimension 0, may hold values from -6 to 6
- value_rows: bfloat16 [4096, 2048], P(('group', 'seq', 'head', 'sub')), parts along dimension 0, may hold values from -6 to 6
- grad_out: bfloat16 [4096, 2048], P(('group', 'seq', 'head', 'sub')), parts along dimension 0, may hold values from -6 to 6
Outputs:
- normed_out: bfloat16 [4096, 2048], P(('group', 'seq', 'head', 'sub')), parts along dimension 0
- grad_query: bfloat16 [4096, 2048], P(('group', 'seq', 'head', 'sub')), parts along dimension 0
- grad_key: bfloat16 [4096, 2048], P(('group', 'seq', 'head', 'sub')), parts along dimension 0
- grad_value: bfloat16 [4096, 2048], P(('group', 'seq', 'head', 'sub')), parts along dimension 0
The draws below stay inside these ranges and needn't reach their ends.
There are 2 independent parts, one for each index of `group`. The reference program is written for one: setup_inputs(seed, part) draws one part's arguments, and reference() takes and returns one part's arrays. A program takes and returns all parts, laid end to end along the dimension named above; each array names one. Nothing has to cross between parts.
All inputs are finite; a program needn't handle non-finite values.
Results may differ from the reference program's by a relative error of at most 0.0059.
Values may be sent and summed in bfloat16 or wider, within the bound.
No kernel may reach another device: no remote copies, remote signals or barrier semaphores. Data moves between devices by JAX's collectives and lax.ppermute only.
A program may use at most 64 MiB of HBM per device.

```python
import jax
import jax.numpy as jnp
from jax import lax

HEADS = 16
HEAD_DIM = 128
BLOCK = 128
TOKENS = 2048


def levels(stream_key, extent, shards, least, largest):
    loudness, own = 1.0, jax.random.fold_in(stream_key, 6)
    for position, blocks in shards:
        draws = jnp.exp(jax.random.uniform(jax.random.fold_in(own, position), (blocks,), jnp.float32, least / len(shards), largest / len(shards)))
        loudness = loudness * jnp.repeat(draws, extent[position] // blocks).reshape([-1 if axis == position else 1 for axis in range(len(extent))])
    return loudness


def noise(key, shape, scale, reach, shards=(), dtype=jnp.bfloat16):
    values = scale * jax.random.normal(key, shape, jnp.float32)
    if shards:
        values = values * levels(key, shape, shards, -0.22, 0.18)
    return jnp.clip(values, -reach, reach).astype(dtype)


def setup_inputs(seed: int = 0, part: int = 0) -> dict:
    arg_keys = jax.random.split(jax.random.key(seed), 5)
    part_splits = jax.random.split(jax.random.fold_in(arg_keys[4], part), 5)
    return {
        "query_rows": noise(part_splits[0], (TOKENS, HEADS * HEAD_DIM), 1.0, 6.0, ((0, 16),)),
        "key_rows": noise(part_splits[1], (TOKENS, HEADS * HEAD_DIM), 1.0, 6.0, ((0, 16),)),
        "value_rows": noise(part_splits[2], (TOKENS, HEADS * HEAD_DIM), 1.0, 6.0, ((0, 16),)),
        "grad_out": noise(part_splits[3], (TOKENS, HEADS * HEAD_DIM), 1.0, 6.0, ((0, 16),)),
    }


EPSILON = 1e-05

def split_blocks(array):
    return array.astype(jnp.float32).reshape(TOKENS // BLOCK, BLOCK, HEADS, HEAD_DIM)

def round_low(array):
    return lax.optimization_barrier(array.astype(jnp.bfloat16)).astype(jnp.float32)

def product(form, left, right):
    return jnp.einsum(form, left, right, precision=lax.Precision.HIGHEST)

def reference(query_rows, key_rows, value_rows, grad_out):
    queries = split_blocks(query_rows)
    key_vals = split_blocks(key_rows)
    value_vals = split_blocks(value_rows)
    cotangent = split_blocks(grad_out)
    causal = jnp.arange(BLOCK)[:, None] >= jnp.arange(BLOCK)[None, :]
    init_state = jnp.zeros((HEADS, HEAD_DIM, HEAD_DIM), jnp.float32)

    def forward_step(carry_state, inputs):
        query_blk, key_blk, value_blk = inputs
        scores = product('the,she->hts', query_blk, key_blk)
        probs = round_low(jnp.where(causal, scores, 0.0))
        state_low = round_low(carry_state)
        unnormed = product('hts,she->the', probs, value_blk) + product('the,hef->thf', query_blk, state_low)
        next_state = carry_state + product('she,shf->hef', key_blk, value_blk)
        return (next_state, (unnormed, state_low))
    final_state, (unnormed, states_low) = lax.scan(forward_step, init_state, (queries, key_vals, value_vals))
    norm_scale = jnp.sqrt(lax.optimization_barrier(jnp.mean(unnormed * unnormed, axis=-1, keepdims=True)) + EPSILON)
    normed = unnormed / norm_scale
    normed_out = normed.astype(jnp.bfloat16).reshape(TOKENS, HEADS * HEAD_DIM)
    grad_raw = (cotangent - normed * lax.optimization_barrier(jnp.mean(cotangent * normed, axis=-1, keepdims=True))) / norm_scale
    grad_low = round_low(grad_raw)

    def backward_step(carry_grad, inputs):
        query_blk, key_blk, value_blk, grad_blk, state_low = inputs
        grad_state = round_low(carry_grad)
        probs = round_low(jnp.where(causal, product('the,she->hts', query_blk, key_blk), 0.0))
        grad_probs = round_low(jnp.where(causal, product('thf,shf->hts', grad_blk, value_blk), 0.0))
        grad_q = product('hts,she->the', grad_probs, key_blk) + product('thf,hef->the', grad_blk, state_low)
        grad_k = product('hts,the->she', grad_probs, query_blk) + product('shf,hef->she', value_blk, grad_state)
        grad_v = product('hts,thf->shf', probs, grad_blk) + product('she,hef->shf', key_blk, grad_state)
        next_grad = carry_grad + product('the,thf->hef', query_blk, grad_blk)
        return (next_grad, (grad_q, grad_k, grad_v))
    final_grad, (grad_q, grad_k, grad_v) = lax.scan(backward_step, init_state, (queries, key_vals, value_vals, grad_low, states_low), reverse=True)
    shape_out = (TOKENS, HEADS * HEAD_DIM)
    return (normed_out, grad_q.astype(jnp.bfloat16).reshape(shape_out), grad_k.astype(jnp.bfloat16).reshape(shape_out), grad_v.astype(jnp.bfloat16).reshape(shape_out))
```

```python
import functools

import jax
import jax.numpy as jnp
from jax import lax
from jax.experimental import pallas as pl
from jax.experimental.pallas import tpu as pltpu
from jax.sharding import PartitionSpec as P

HEAD_DIM = 128
BLOCK = 128
EPSILON = 1e-05
BF = jnp.bfloat16
F32 = jnp.float32
NN = (((1,), (0,)), ((), ()))
NT = (((1,), (1,)), ((), ()))
TN = (((0,), (0,)), ((), ()))


def dot(left, right, form):
    return lax.dot_general(left, right, form, preferred_element_type=F32)


def causal_mask():
    rows = lax.broadcasted_iota(jnp.int32, (BLOCK, BLOCK), 0)
    cols = lax.broadcasted_iota(jnp.int32, (BLOCK, BLOCK), 1)
    return rows >= cols


def columns(slot, flip_ref):
    head = lax.bitwise_xor(jnp.int32(slot), flip_ref[0])
    return pl.ds(pl.multiple_of(head * HEAD_DIM, HEAD_DIM), HEAD_DIM)


def key_value_body(heads, flip_ref, k_ref, v_ref, send_ref, keep_ref):
    half = heads // 2
    for slot in list(range(half, heads)) + list(range(half)):
        at = columns(slot, flip_ref)
        state = dot(k_ref[:, at], v_ref[:, at], TN)
        if slot >= half:
            send_ref[slot - half] = state.astype(BF)
        else:
            keep_ref[slot] = state


def inner_body(heads, q_ref, k_ref, v_ref, probs_ref, inner_ref):
    mask = causal_mask()
    for head in range(heads):
        at = pl.ds(head * HEAD_DIM, HEAD_DIM)
        probs = jnp.where(mask, dot(q_ref[:, at], k_ref[:, at], NT), 0.0).astype(BF)
        probs_ref[head] = probs
        inner_ref[:, at] = dot(probs, v_ref[:, at], NN)


def norm_body(
    heads, flip_ref, q_ref, g_ref, inner_ref, near_ref, far_ref, normed_ref, raw_ref, send_ref, keep_ref
):
    half = heads // 2
    for slot in list(range(half, heads)) + list(range(half)):
        at = columns(slot, flip_ref)
        query = q_ref[:, at]
        state = far_ref[slot - half] if slot >= half else near_ref[slot]
        unnormed = inner_ref[:, at] + dot(query, state, NN)
        inv = lax.rsqrt(jnp.mean(unnormed * unnormed, axis=-1, keepdims=True) + EPSILON)
        normed = unnormed * inv
        normed_ref[:, at] = normed.astype(BF)
        cot = g_ref[:, at].astype(F32)
        raw = (cot - normed * jnp.mean(cot * normed, axis=-1, keepdims=True)) * inv
        raw = raw.astype(BF)
        raw_ref[:, at] = raw
        grad = dot(query, raw, TN)
        if slot >= half:
            send_ref[slot - half] = grad.astype(BF)
        else:
            keep_ref[slot] = grad


def local_grads_body(
    heads, flip_ref, q_ref, k_ref, v_ref, raw_ref, probs_ref, near_ref, far_ref, gq_ref, gk_ref, gv_ref
):
    half = heads // 2
    mask = causal_mask()
    for slot in range(heads):
        at = columns(slot, flip_ref)
        head = lax.bitwise_xor(jnp.int32(slot), flip_ref[0])
        raw = raw_ref[:, at]
        state = far_ref[slot - half] if slot >= half else near_ref[slot]
        grad_probs = jnp.where(mask, dot(raw, v_ref[:, at], NT), 0.0).astype(BF)
        gq_ref[:, at] = (dot(grad_probs, k_ref[:, at], NN) + dot(raw, state, NT)).astype(BF)
        gk_ref[:, at] = dot(grad_probs, q_ref[:, at], TN)
        gv_ref[:, at] = dot(probs_ref[head], raw, TN)


def last_grads_body(
    heads, flip_ref, k_ref, v_ref, gk_in_ref, gv_in_ref, near_ref, far_ref, gk_ref, gv_ref
):
    half = heads // 2
    for slot in range(heads):
        at = columns(slot, flip_ref)
        state = far_ref[slot - half] if slot >= half else near_ref[slot]
        gk_ref[:, at] = (gk_in_ref[:, at] + dot(v_ref[:, at], state, NT)).astype(BF)
        gv_ref[:, at] = (gv_in_ref[:, at] + dot(k_ref[:, at], state, NN)).astype(BF)


def call(body, flip, arrays, outs, flops):
    in_specs = [pl.BlockSpec(memory_space=pltpu.VMEM)] * len(arrays)
    operands = list(arrays)
    if flip is not None:
        in_specs = [pl.BlockSpec(memory_space=pltpu.SMEM)] + in_specs
        operands = [flip] + operands
    size = sum(a.size * a.dtype.itemsize for a in arrays)
    size += sum(o.size * o.dtype.itemsize for o in outs)
    return pl.pallas_call(
        body,
        out_shape=outs,
        in_specs=in_specs,
        out_specs=[pl.BlockSpec(memory_space=pltpu.VMEM)] * len(outs),
        compiler_params=pltpu.CompilerParams(vmem_limit_bytes=24 * 1024 * 1024),
        cost_estimate=pl.CostEstimate(flops=flops, bytes_accessed=size, transcendentals=0),
    )(*operands)


def swap(value, axis, bit):
    pairs = [(i, i ^ bit) for i in range(lax.axis_size(axis))]
    return lax.ppermute(value, axis, pairs)


def bits_of(axis):
    return [1 << b for b in range(lax.axis_size(axis).bit_length() - 1)]


def has_bit(axis, bit):
    return (lax.axis_index(axis) & bit) != 0


def scan_states(send, keep, reverse):
    levels = [(axis, bit) for axis in ("sub", "head") for bit in bits_of(axis)]
    zero = jnp.zeros((), F32)
    total, saved = keep, []
    for number, (axis, bit) in enumerate(levels):
        if number:
            half = total.shape[0] // 2
            send, total = total[half:].astype(BF), total[:half]
        got = swap(send, axis, bit).astype(F32)
        saved.append((axis, bit, total, got))
        total = total + got
    carried = jnp.zeros_like(total)
    for bit in bits_of("seq"):
        got = swap(total.astype(BF), "seq", bit).astype(F32)
        counts = has_bit("seq", bit) != reverse
        carried = carried + jnp.where(counts, got, zero)
        total = total + got
    for number, (axis, bit, own, got) in reversed(list(enumerate(saved))):
        counts = has_bit(axis, bit) != reverse
        message = (carried + jnp.where(counts, zero, own)).astype(BF)
        near = carried + jnp.where(counts, got, zero)
        far = swap(message, axis, bit)
        if number:
            carried = jnp.concatenate([near, far.astype(F32)], axis=0)
    return near.astype(BF), far


def on_device(query, key, value, cot):
    rows, width = query.shape
    heads = width // HEAD_DIM
    half = heads // 2
    flip = jnp.zeros((), jnp.int32)
    weight = half
    for axis in ("sub", "head"):
        for bit in bits_of(axis):
            flip = flip + jnp.where(has_bit(axis, bit), weight, 0).astype(jnp.int32)
            weight //= 2
    flip = flip.reshape(1)
    state = (half, HEAD_DIM, HEAD_DIM)
    unit = 2 * BLOCK * HEAD_DIM * HEAD_DIM * heads

    def shape(dims, dtype):
        return jax.ShapeDtypeStruct(dims, dtype)

    send, keep = call(
        functools.partial(key_value_body, heads), flip, (key, value),
        [shape(state, BF), shape(state, F32)], unit,
    )
    probs, inner = call(
        functools.partial(inner_body, heads), None, (query, key, value),
        [shape((heads, BLOCK, BLOCK), BF), shape((rows, width), F32)], 2 * unit,
    )
    near, far = scan_states(send, keep, False)
    normed, raw, send, keep = call(
        functools.partial(norm_body, heads), flip, (query, cot, inner, near, far),
        [shape((rows, width), BF), shape((rows, width), BF), shape(state, BF), shape(state, F32)], 2 * unit,
    )
    grad_q, grad_k, grad_v = call(
        functools.partial(local_grads_body, heads), flip, (query, key, value, raw, probs, near, far),
        [shape((rows, width), BF), shape((rows, width), F32), shape((rows, width), F32)], 5 * unit,
    )
    near, far = scan_states(send, keep, True)
    grad_k, grad_v = call(
        functools.partial(last_grads_body, heads), flip, (key, value, grad_k, grad_v, near, far),
        [shape((rows, width), BF), shape((rows, width), BF)], 2 * unit,
    )
    return normed, grad_q, grad_k, grad_v


def solution(mesh):
    placed = P(("group", "seq", "head", "sub"), None)
    return jax.shard_map(
        on_device,
        mesh=mesh,
        in_specs=(placed,) * 4,
        out_specs=(placed,) * 4,
        check_vma=False,
    )
```

```python
import functools

import jax
import jax.numpy as jnp
from jax import lax
from jax.experimental import pallas as pl
from jax.experimental.pallas import tpu as pltpu
from jax.sharding import PartitionSpec as P

HEAD_DIM = 128
BLOCK = 128
EPSILON = 1e-05
STREAMS = 2
BF = jnp.bfloat16
F32 = jnp.float32
NN = (((1,), (0,)), ((), ()))
NT = (((1,), (1,)), ((), ()))
TN = (((0,), (0,)), ((), ()))


def dot(left, right, form):
    return lax.dot_general(left, right, form, preferred_element_type=F32)


def causal_mask():
    rows = lax.broadcasted_iota(jnp.int32, (BLOCK, BLOCK), 0)
    cols = lax.broadcasted_iota(jnp.int32, (BLOCK, BLOCK), 1)
    return rows >= cols


AXES = ("seq", "head", "sub")


def place_bit(level):
    place = lax.axis_index(AXES).astype(jnp.int32)
    return lax.bitwise_and(lax.shift_right_logical(place, jnp.int32(level)), jnp.int32(1))


class Stream:
    def __init__(self, number, heads, plane):
        self.number, self.slots = number, heads // STREAMS
        self.kept = heads // plane
        self.run = self.kept // STREAMS
        self.halvings = [heads >> (level + 1) for level in range(plane.bit_length() - 1)]

    def start(self, slot, width):
        position = (slot // self.run) * self.kept + self.number * self.run + slot % self.run
        head = jnp.int32(position)
        for level, weight in enumerate(self.halvings):
            head = lax.bitwise_xor(head, place_bit(level) * weight)
        return pl.ds(pl.multiple_of(head * HEAD_DIM, HEAD_DIM), width * HEAD_DIM)

    def columns(self, slot):
        return self.start(slot, 1)


def key_value_body(streams, k_ref, v_ref, *rest):
    *pairs, bits_ref, k_out, v_out, sems = rest
    half, run = streams[0].slots // 2, streams[0].run
    groups = streams[0].slots // run
    order = [
        (stream, group)
        for stream in streams
        for group in list(range(groups // 2, groups)) + list(range(groups // 2))
    ]
    copies = []
    for number, (stream, group) in enumerate(order):
        at = stream.start(group * run, run)
        copies.append([
            pltpu.make_async_copy(k_ref.at[:, at], k_out.at[:, at], sems.at[0, number]),
            pltpu.make_async_copy(v_ref.at[:, at], v_out.at[:, at], sems.at[1, number]),
        ])
        for copy in copies[-1]:
            copy.start()
    for level in range(bits_ref.shape[0]):
        bits_ref[level] = jnp.full(bits_ref.shape[1:], place_bit(level).astype(F32), F32)
    for (stream, group), pair in zip(order, copies):
        send_ref, keep_ref = pairs[2 * stream.number : 2 * stream.number + 2]
        for copy in pair:
            copy.wait()
        for slot in range(group * run, (group + 1) * run):
            at = stream.columns(slot)
            state = dot(k_out[:, at], v_out[:, at], TN)
            if slot >= half:
                send_ref[slot - half] = state.astype(BF)
            else:
                keep_ref[slot] = state


def inner_body(stream, q_ref, k_ref, v_ref, probs_ref, inner_ref):
    mask = causal_mask()
    for slot in range(stream.slots):
        at = stream.columns(slot)
        probs = jnp.where(mask, dot(q_ref[:, at], k_ref[:, at], NT), 0.0).astype(BF)
        probs_ref[slot] = probs
        inner_ref[slot] = dot(probs, v_ref[:, at], NN)


def norm_body(stream, base, q_ref, g_ref, inner_ref, state_ref, normed_ref, raw_ref, grad_ref):
    for number in range(state_ref.shape[0]):
        at = stream.columns(base + number)
        query = q_ref[:, at]
        unnormed = inner_ref[base + number] + dot(query, state_ref[number], NN)
        inv = lax.rsqrt(jnp.mean(unnormed * unnormed, axis=-1, keepdims=True) + EPSILON)
        normed = unnormed * inv
        normed_ref[number] = normed.astype(BF)
        cot = g_ref[:, at].astype(F32)
        raw = (cot - normed * jnp.mean(cot * normed, axis=-1, keepdims=True)) * inv
        raw = raw.astype(BF)
        raw_ref[number] = raw
        grad_ref[number] = dot(query, raw, TN).astype(grad_ref.dtype)


def local_grads_body(stream, q_ref, k_ref, v_ref, probs_ref, *rest):
    near_refs, far_refs, rest = rest[:3], rest[3:6], rest[6:]
    *_, gk_ref, gv_ref, normed_out, gq_out, gq_buf, sems = rest
    half = stream.slots // 2
    mask = causal_mask()
    copies = []
    held = [
        tuple(ref.at[slot % half] for ref in (near_refs, far_refs)[slot // half])
        for slot in range(stream.slots)
    ]
    for slot in range(stream.slots):
        at = stream.columns(slot)
        copies.append(
            pltpu.make_async_copy(held[slot][0], normed_out.at[:, at], sems.at[0, slot])
        )
        copies[-1].start()
    for slot in range(stream.slots):
        at = stream.columns(slot)
        raw, state = held[slot][1][...], held[slot][2][...]
        grad_probs = jnp.where(mask, dot(raw, v_ref[:, at], NT), 0.0).astype(BF)
        gq_buf[slot] = (dot(grad_probs, k_ref[:, at], NN) + dot(raw, state, NT)).astype(BF)
        copies.append(
            pltpu.make_async_copy(gq_buf.at[slot], gq_out.at[:, at], sems.at[1, slot])
        )
        copies[-1].start()
        gk_ref[slot] = dot(grad_probs, q_ref[:, at], TN)
        gv_ref[slot] = dot(probs_ref[slot], raw, TN)
    for copy in copies:
        copy.wait()


def last_grads_body(streams, base, k_ref, v_ref, *rest):
    parts = [rest[3 * s : 3 * s + 3] for s in range(len(streams))]
    *_, gk_out, gv_out, gk_buf, gv_buf, sems = rest
    copies = []
    for stream, (gk_ref, gv_ref, state_ref) in zip(streams, parts):
        for number in range(state_ref.shape[0]):
            slot, at = base + number, stream.columns(base + number)
            state, to = state_ref[number], (stream.number, number)
            gk_buf[to] = (gk_ref[slot] + dot(v_ref[:, at], state, NT)).astype(BF)
            copies.append(pltpu.make_async_copy(gk_buf.at[to], gk_out.at[:, at], sems.at[0, *to]))
            copies[-1].start()
            gv_buf[to] = (gv_ref[slot] + dot(k_ref[:, at], state, NN)).astype(BF)
            copies.append(pltpu.make_async_copy(gv_buf.at[to], gv_out.at[:, at], sems.at[1, *to]))
            copies[-1].start()
    for copy in copies:
        copy.wait()


def hbm(shape, dtype):
    return jax.ShapeDtypeStruct(shape, dtype)


def call(body, arrays, outs, flops, scratch=(), raw_in=False, partial=()):
    if raw_in:
        arrays = [pltpu.with_memory_space_constraint(a, pltpu.HBM) for a in arrays]
    vmem, anywhere = pl.BlockSpec(memory_space=pltpu.VMEM), pl.BlockSpec(memory_space=pl.ANY)
    operands = [*arrays, *partial]
    in_specs = [pl.BlockSpec(memory_space=pltpu.HBM) if raw_in else vmem] * len(arrays) + [anywhere] * len(partial)
    whole = [isinstance(out, jax.ShapeDtypeStruct) for out in outs]
    first = whole.index(True) if True in whole else 0
    aliases = {len(arrays) + i: first + i for i in range(len(partial))}
    size = sum(a.size * a.dtype.itemsize for a in arrays) * 2
    return pl.pallas_call(
        body,
        out_shape=outs,
        in_specs=in_specs,
        out_specs=[anywhere if w else vmem for w in whole],
        scratch_shapes=list(scratch),
        input_output_aliases=aliases,
        compiler_params=pltpu.CompilerParams(vmem_limit_bytes=8 * 1024 * 1024),
        cost_estimate=pl.CostEstimate(flops=flops, bytes_accessed=size, transcendentals=0),
    )(*operands)


def swap(value, axis, bit):
    pairs = [(i, i ^ bit) for i in range(lax.axis_size(axis))]
    return lax.ppermute(value, axis, pairs)


def bits_of(axis):
    return [1 << b for b in range(lax.axis_size(axis).bit_length() - 1)]


def gated(value, bits, level, wanted):
    return jnp.where(bits[level, :1][None] == wanted, value, 0.0)


def scan_states(sends, keeps, bits, reverse, asides):
    levels = [(axis, bit) for axis in ("sub", "head") for bit in bits_of(axis)]
    streams = range(len(sends))
    upper, lower = (0.0, 1.0) if reverse else (1.0, 0.0)
    sends, totals, saved = list(sends), list(keeps), []
    given = {}

    def exchange(value, axis, bit, at):
        if at not in asides:
            return swap(value, axis, bit).astype(F32)
        work, operands = asides[at]
        value, operands = lax.optimization_barrier((value, operands))
        got, given[at] = lax.optimization_barrier((swap(value, axis, bit), work(operands)))
        return got.astype(F32)

    for number, (axis, bit) in enumerate(levels):
        row = []
        for s in streams:
            if number:
                half = totals[s].shape[0] // 2
                sends[s], totals[s] = totals[s][half:].astype(BF), totals[s][:half]
            got = exchange(sends[s], axis, bit, (number, s))
            row.append((totals[s], got))
            totals[s] = totals[s] + got
        saved.append((axis, bit, row))
    carried = [jnp.zeros_like(total) for total in totals]
    for number, bit in enumerate(bits_of("seq"), len(levels)):
        for s in streams:
            got = exchange(totals[s].astype(BF), "seq", bit, (number, s))
            carried[s] = carried[s] + gated(got, bits, number, upper)
            totals[s] = totals[s] + got
    near, far = [None] * len(sends), [None] * len(sends)
    for number, (axis, bit, row) in reversed(list(enumerate(saved))):
        for s in streams:
            own, got = row[s]
            message = (carried[s] + gated(own, bits, number, lower)).astype(BF)
            known = carried[s] + gated(got, bits, number, upper)
            near[s], far[s] = known.astype(BF), swap(message, axis, bit)
            if number:
                carried[s] = jnp.concatenate([known, far[s].astype(F32)], axis=0)
    return near, far, given


def spread(streams):
    plane = len(bits_of("sub")) + len(bits_of("head"))
    return [(plane - 1 + stream.number, STREAMS - 1) for stream in streams]


def on_device(query, key, value, cot):
    rows, width = query.shape
    heads = width // HEAD_DIM
    plane = lax.axis_size("head") * lax.axis_size("sub")
    levels = lax.axis_size(AXES).bit_length() - 1
    streams = [Stream(s, heads, plane) for s in range(STREAMS)]
    count, slots, half = len(streams), streams[0].slots, streams[0].slots // 2
    half_state = (half, HEAD_DIM, HEAD_DIM)
    full_state = (slots, HEAD_DIM, HEAD_DIM)
    unit = 2 * BLOCK * HEAD_DIM * HEAD_DIM * slots
    vm, dma = pltpu.VMEM, pltpu.SemaphoreType.DMA

    *states, bits, key_vm, value_vm = call(
        functools.partial(key_value_body, streams), (key, value),
        [vm(half_state, BF), vm(half_state, F32)] * count
        + [vm((levels, 8, HEAD_DIM), F32), vm((rows, width), BF), vm((rows, width), BF)],
        unit * count, (dma((2, heads // streams[0].run)),), raw_in=True,
    )
    def inner_work(stream, operands):
        return call(
            functools.partial(inner_body, stream), operands,
            [vm(full_state, BF), vm(full_state, F32)], 2 * unit,
        )

    spots = spread(streams)
    near, far, inner = scan_states(
        states[0::2], states[1::2], bits, False,
        {
            spot: (functools.partial(inner_work, stream), (query, key_vm, value_vm))
            for spot, stream in zip(spots, streams)
        },
    )
    inner = [inner[spot] for spot in spots]

    def norm(s, base, state, dtype):
        return call(
            functools.partial(norm_body, streams[s], base), (query, cot, inner[s][1], state),
            [vm(half_state, BF), vm(half_state, BF), vm(half_state, dtype)], unit,
        )

    normed_near, normed_far = [], []
    for s in range(count):
        normed_near.append(norm(s, 0, near[s], F32))
        far[s], normed_near[s] = lax.optimization_barrier((far[s], normed_near[s]))
        normed_far.append(norm(s, half, far[s], BF))
    partials = ()

    def local_grads(stream, operands):
        nonlocal partials
        out = call(
            functools.partial(local_grads_body, stream), operands,
            [vm(full_state, F32), vm(full_state, F32), hbm((rows, width), BF), hbm((rows, width), BF)],
            5 * unit, (vm(full_state, BF), dma((2, slots))), partial=partials,
        )
        partials = out[2:]
        return out[:2]

    near, far, outs = scan_states(
        [n[2] for n in normed_far], [n[2] for n in normed_near], bits, True,
        {
            spot: (
                functools.partial(local_grads, stream),
                (query, key_vm, value_vm, inner[s][0], *normed_near[s][:2], near[s], *normed_far[s][:2], far[s]),
            )
            for s, (spot, stream) in enumerate(zip(spots, streams))
        },
    )
    outs = [outs[spot] for spot in spots]
    normed_out, grad_q = partials
    partials = ()
    for base in (0, half):
        found = far if base else near
        buf = vm((count, *half_state), BF)
        operands = [a for s in range(count) for a in (*outs[s], found[s])]
        partials = call(
            functools.partial(last_grads_body, streams, base), (key_vm, value_vm, *operands),
            [hbm((rows, width), BF), hbm((rows, width), BF)], 2 * unit,
            (buf, buf, dma((2, count, half))), partial=partials,
        )
        if base == 0:
            far, partials = lax.optimization_barrier((far, partials))
    grad_k, grad_v = partials
    return normed_out, grad_q, grad_k, grad_v


def solution(mesh):
    placed = P(("group", "seq", "head", "sub"), None)
    return jax.shard_map(
        on_device,
        mesh=mesh,
        in_specs=(placed,) * 4,
        out_specs=(placed,) * 4,
        check_vma=False,
    )
```

```python
import functools

import jax
import jax.numpy as jnp
from jax import lax
from jax.experimental import pallas as pl
from jax.experimental.pallas import tpu as pltpu
from jax.sharding import PartitionSpec as P

HEAD_DIM = 128
BLOCK = 128
EPSILON = 1e-05
BF = jnp.bfloat16
F32 = jnp.float32
NN = (((1,), (0,)), ((), ()))
NT = (((1,), (1,)), ((), ()))
TN = (((0,), (0,)), ((), ()))
AXES = ("seq", "head", "sub")


def dot(left, right, form):
    return lax.dot_general(left, right, form, preferred_element_type=F32)


def causal_mask():
    rows = lax.broadcasted_iota(jnp.int32, (BLOCK, BLOCK), 0)
    cols = lax.broadcasted_iota(jnp.int32, (BLOCK, BLOCK), 1)
    return rows >= cols


def place_bit(level):
    place = lax.axis_index(AXES).astype(jnp.int32)
    return lax.bitwise_and(lax.shift_right_logical(place, jnp.int32(level)), jnp.int32(1))


def bits_in(axis):
    return lax.axis_size(axis).bit_length() - 1


class Plan:
    def __init__(self, heads):
        self.heads, self.half = heads, heads // 2
        self.steps = bits_in("head") + (bits_in("seq") > 0)
        self.groups = 1 << self.steps
        self.kept = self.half // self.groups
        self.part = self.half // 2

    def columns(self, slot, width=1):
        head = jnp.int32(slot)
        for level in range(self.steps + 1):
            head = lax.bitwise_xor(head, place_bit(level) * (self.heads >> (level + 1)))
        return pl.ds(pl.multiple_of(head * HEAD_DIM, HEAD_DIM), width * HEAD_DIM)

    def mask(self, group):
        return sum(((group >> (self.steps - 1 - j)) & 1) << j for j in range(self.steps))

    def base(self, part, far):
        return far * self.half + (1 - part) * self.part


def key_value_body(plan, k_ref, v_ref, *rest):
    *parts, bits_ref, k_out, v_out, sems = rest
    order = [(part, far) for far in (1, 0) for part in (0, 1)]
    copies = {}
    for part, far in order:
        for first in range(plan.base(part, far), plan.base(part, far) + plan.part, plan.kept):
            at, number = plan.columns(first, plan.kept), first // plan.kept
            copies[first] = [
                pltpu.make_async_copy(k_ref.at[:, at], k_out.at[:, at], sems.at[0, number]),
                pltpu.make_async_copy(v_ref.at[:, at], v_out.at[:, at], sems.at[1, number]),
            ]
            for copy in copies[first]:
                copy.start()
    for level in range(bits_ref.shape[0]):
        bits_ref[level] = jnp.full(bits_ref.shape[1:], place_bit(level).astype(F32), F32)
    for (part, far), out_ref in zip(order, parts):
        for number in range(plan.part):
            slot = plan.base(part, far) + number
            for copy in copies.get(slot, ()):
                copy.wait()
            at = plan.columns(slot)
            out_ref[number] = dot(k_out[:, at], v_out[:, at], TN).astype(out_ref.dtype)


def inner_body(plan, base, q_ref, k_ref, v_ref, probs_ref, inner_ref):
    mask = causal_mask()
    for number in range(plan.half):
        at = plan.columns(base + number)
        probs = jnp.where(mask, dot(q_ref[:, at], k_ref[:, at], NT), 0.0).astype(BF)
        probs_ref[number] = probs
        inner_ref[number] = dot(probs, v_ref[:, at], NN)


def norm_body(plan, base, q_ref, g_ref, inner_ref, state_ref, normed_ref, raw_ref, grad_ref):
    for number in range(plan.part):
        at = plan.columns(base + number)
        query = q_ref[:, at]
        unnormed = inner_ref[base % plan.half + number] + dot(query, state_ref[number], NN)
        inv = lax.rsqrt(jnp.mean(unnormed * unnormed, axis=-1, keepdims=True) + EPSILON)
        normed = unnormed * inv
        normed_ref[number] = normed.astype(BF)
        cot = g_ref[:, at].astype(F32)
        raw = (cot - normed * jnp.mean(cot * normed, axis=-1, keepdims=True)) * inv
        raw = raw.astype(BF)
        raw_ref[number] = raw
        grad_ref[number] = dot(query, raw, TN).astype(grad_ref.dtype)


def local_grads_body(plan, far, q_ref, k_ref, v_ref, probs_ref, *rest):
    upper, lower, rest = rest[:3], rest[3:6], rest[6:]
    *_, gk_ref, gv_ref, normed_out, gq_out, gq_buf, sems = rest
    mask = causal_mask()
    copies, held = [], {}
    for part, refs in enumerate((upper, lower)):
        for number in range(plan.part):
            slot = plan.base(part, far) + number
            held[slot] = [ref.at[number] for ref in refs]
    for slot, (normed_ref, _, _) in held.items():
        at, number = plan.columns(slot), slot % plan.half
        copies.append(pltpu.make_async_copy(normed_ref, normed_out.at[:, at], sems.at[0, number]))
        copies[-1].start()
    for slot, (_, raw_ref, state_ref) in held.items():
        at, number = plan.columns(slot), slot % plan.half
        raw, state = raw_ref[...], state_ref[...]
        grad_probs = jnp.where(mask, dot(raw, v_ref[:, at], NT), 0.0).astype(BF)
        gq_buf[number] = (dot(grad_probs, k_ref[:, at], NN) + dot(raw, state, NT)).astype(BF)
        copies.append(pltpu.make_async_copy(gq_buf.at[number], gq_out.at[:, at], sems.at[1, number]))
        copies[-1].start()
        gk_ref[number] = dot(grad_probs, q_ref[:, at], TN)
        gv_ref[number] = dot(probs_ref[number], raw, TN)
    for copy in copies:
        copy.wait()


def last_grads_body(plan, far, k_ref, v_ref, gk_ref, gv_ref, *rest):
    states = rest[:2]
    *_, gk_out, gv_out, gk_buf, gv_buf, sems = rest
    copies = []
    for part, state_ref in enumerate(states):
        for inside in range(plan.part):
            slot = plan.base(part, far) + inside
            at, number = plan.columns(slot), slot % plan.half
            state = state_ref[inside]
            gk_buf[number] = (gk_ref[number] + dot(v_ref[:, at], state, NT)).astype(BF)
            copies.append(
                pltpu.make_async_copy(gk_buf.at[number], gk_out.at[:, at], sems.at[0, number])
            )
            copies[-1].start()
            gv_buf[number] = (gv_ref[number] + dot(k_ref[:, at], state, NN)).astype(BF)
            copies.append(
                pltpu.make_async_copy(gv_buf.at[number], gv_out.at[:, at], sems.at[1, number])
            )
            copies[-1].start()
    for copy in copies:
        copy.wait()


def hbm(shape, dtype):
    return jax.ShapeDtypeStruct(shape, dtype)


def call(body, arrays, outs, flops, scratch=(), raw_in=False, partial=()):
    if raw_in:
        arrays = [pltpu.with_memory_space_constraint(a, pltpu.HBM) for a in arrays]
    vmem, anywhere = pl.BlockSpec(memory_space=pltpu.VMEM), pl.BlockSpec(memory_space=pl.ANY)
    operands = [*arrays, *partial]
    in_specs = [pl.BlockSpec(memory_space=pltpu.HBM) if raw_in else vmem] * len(arrays) + [anywhere] * len(partial)
    whole = [isinstance(out, jax.ShapeDtypeStruct) for out in outs]
    first = whole.index(True) if True in whole else 0
    aliases = {len(arrays) + i: first + i for i in range(len(partial))}
    size = sum(a.size * a.dtype.itemsize for a in arrays) * 2
    return pl.pallas_call(
        body,
        out_shape=outs,
        in_specs=in_specs,
        out_specs=[anywhere if w else vmem for w in whole],
        scratch_shapes=list(scratch),
        input_output_aliases=aliases,
        compiler_params=pltpu.CompilerParams(vmem_limit_bytes=8 * 1024 * 1024),
        cost_estimate=pl.CostEstimate(flops=flops, bytes_accessed=size, transcendentals=0),
    )(*operands)


def swap(value, axes, mask):
    pairs = [(i, i ^ mask) for i in range(lax.axis_size(axes))]
    return lax.ppermute(value, axes, pairs)


def gated(value, bits, level, wanted):
    return jnp.where(bits[level, :1][None] == wanted, value, 0.0)


def before(own, others, target, bits, reverse):
    total = None
    for mask, state in ((0, own), *others.items()):
        if mask != target:
            step = (mask ^ target).bit_length() - 1
            wanted = 1.0 - ((target >> step) & 1)
            term = gated(state, bits, step + 1, 1.0 - wanted if reverse else wanted)
            total = term if total is None else total + term
    return total


def scan_states(plan, sends, keeps, bits, reverse, asides):
    chips = ("seq", "head")
    upper, lower = (0.0, 1.0) if reverse else (1.0, 0.0)
    given = {}

    def beside(name, value, axes, mask):
        if name not in asides:
            return swap(value, axes, mask)
        work, operands = asides[name]
        value, operands = lax.optimization_barrier((value, operands))
        got, given[name] = lax.optimization_barrier((swap(value, axes, mask), work(operands)))
        return got

    share = plan.groups // 2
    members = [range(share, plan.groups), range(share)]
    own, near_got, pair = {}, {}, {}
    for part, (send, keep) in enumerate(zip(sends, keeps)):
        got = swap(send, "sub", 1)
        for number, group in enumerate(members[part]):
            rows = slice(number * plan.kept, (number + 1) * plan.kept)
            own[group], near_got[group] = keep[rows], got[rows].astype(F32)
            pair[group] = own[group] + near_got[group]
    order = [group for part in members for group in part if group]
    others = {}
    for group in order:
        name = "share" if group == order[-1] else ""
        got = beside(name, pair[group].astype(BF), chips, plan.mask(group))
        others[plan.mask(group)] = got.astype(F32)
    total = pair[0]
    for state in others.values():
        total = total + state
    carried = jnp.zeros_like(total)
    for level in range(plan.steps, bits_in(chips)):
        name = "total" if level == bits_in(chips) - 1 else ""
        got = beside(name, total.astype(BF), chips, 1 << level).astype(F32)
        carried = carried + gated(got, bits, level + 1, upper)
        total = total + got
    sums = {0: carried + before(pair[0], others, 0, bits, reverse)}
    for group in order:
        message = carried + before(pair[0], others, plan.mask(group), bits, reverse)
        sums[group] = swap(message.astype(BF), chips, plan.mask(group)).astype(F32)
    near, far = [], []
    for part in members:
        message = [sums[group] + gated(own[group], bits, 0, lower) for group in part]
        known = [sums[group] + gated(near_got[group], bits, 0, upper) for group in part]
        far.append(swap(jnp.concatenate(message).astype(BF), "sub", 1))
        near.append(jnp.concatenate(known).astype(BF))
    return near, far, given


def on_device(query, key, value, cot):
    rows, width = query.shape
    plan = Plan(width // HEAD_DIM)
    levels = bits_in(AXES)
    part_state = (plan.part, HEAD_DIM, HEAD_DIM)
    half_state = (plan.half, HEAD_DIM, HEAD_DIM)
    unit = 2 * BLOCK * HEAD_DIM * HEAD_DIM * plan.half
    vm, dma = pltpu.VMEM, pltpu.SemaphoreType.DMA
    whole = hbm((rows, width), BF)

    *states, bits, key_vm, value_vm = call(
        functools.partial(key_value_body, plan), (key, value),
        [vm(part_state, BF)] * 2 + [vm(part_state, F32)] * 2
        + [vm((levels, 8, HEAD_DIM), F32), vm((rows, width), BF), vm((rows, width), BF)],
        unit * 2, (dma((2, plan.heads // plan.kept)),), raw_in=True,
    )

    def inner_work(far, operands):
        return call(
            functools.partial(inner_body, plan, far * plan.half), operands,
            [vm(half_state, BF), vm(half_state, F32)], 2 * unit,
        )

    near, far, given = scan_states(
        plan, states[:2], states[2:], bits, False,
        {
            "share": (functools.partial(inner_work, 0), (query, key_vm, value_vm)),
            "total": (functools.partial(inner_work, 1), (query, key_vm, value_vm)),
        },
    )
    inner = [given["share"], given["total"]]

    def norm(part, is_far, state):
        return call(
            functools.partial(norm_body, plan, plan.base(part, is_far)),
            (query, cot, inner[is_far][1], state),
            [vm(part_state, BF), vm(part_state, BF), vm(part_state, BF if is_far else F32)], unit,
        )

    normed = [[], []]
    for part in range(2):
        normed[0].append(norm(part, 0, near[part]))
        far[part], normed[0][part] = lax.optimization_barrier((far[part], normed[0][part]))
    for part in range(2):
        normed[1].append(norm(part, 1, far[part]))
    partials = ()

    def local_grads(is_far, operands):
        nonlocal partials
        out = call(
            functools.partial(local_grads_body, plan, is_far), operands,
            [vm(half_state, F32), vm(half_state, F32), whole, whole],
            5 * unit, (vm(half_state, BF), dma((2, plan.half))), partial=partials,
        )
        partials = out[2:]
        return out[:2]

    def operands(is_far, found):
        parts = [a for part in range(2) for a in (*normed[is_far][part][:2], found[part])]
        return (query, key_vm, value_vm, inner[is_far][0], *parts)

    near, far, given = scan_states(
        plan, [n[2] for n in normed[1]], [n[2] for n in normed[0]], bits, True,
        {
            "share": (functools.partial(local_grads, 0), operands(0, near)),
            "total": (functools.partial(local_grads, 1), operands(1, far)),
        },
    )
    grads = [given["share"], given["total"]]
    normed_out, grad_q = partials
    partials = ()
    for is_far in range(2):
        found = far if is_far else near
        buf = vm(half_state, BF)
        partials = call(
            functools.partial(last_grads_body, plan, is_far), (key_vm, value_vm, *grads[is_far], *found),
            [whole, whole], 2 * unit, (buf, buf, dma((2, plan.half))), partial=partials,
        )
        if not is_far:
            far, partials = lax.optimization_barrier((far, partials))
    grad_k, grad_v = partials
    return normed_out, grad_q, grad_k, grad_v


def solution(mesh):
    placed = P(("group", "seq", "head", "sub"), None)
    return jax.shard_map(
        on_device,
        mesh=mesh,
        in_specs=(placed,) * 4,
        out_specs=(placed,) * 4,
        check_vma=False,
    )
```

```python
import functools

import jax
import jax.numpy as jnp
from jax import lax
from jax.experimental import pallas as pl
from jax.experimental.pallas import tpu as pltpu
from jax.sharding import PartitionSpec as P

HEAD_DIM = 128
BLOCK = 128
EPSILON = 1e-05
BF = jnp.bfloat16
F32 = jnp.float32
NN = (((1,), (0,)), ((), ()))
NT = (((1,), (1,)), ((), ()))
TN = (((0,), (0,)), ((), ()))
AXES = ("seq", "head", "sub")


def dot(left, right, form):
    return lax.dot_general(left, right, form, preferred_element_type=F32)


def causal_mask():
    rows = lax.broadcasted_iota(jnp.int32, (BLOCK, BLOCK), 0)
    cols = lax.broadcasted_iota(jnp.int32, (BLOCK, BLOCK), 1)
    return rows >= cols


def place_bit(level):
    place = lax.axis_index(AXES).astype(jnp.int32)
    return lax.bitwise_and(lax.shift_right_logical(place, jnp.int32(level)), jnp.int32(1))


def bits_in(axis):
    return lax.axis_size(axis).bit_length() - 1


class Plan:
    def __init__(self, heads):
        self.heads, self.half = heads, heads // 2
        self.steps = bits_in("head") + (bits_in("seq") > 0)
        self.groups = 1 << self.steps
        self.kept = self.half // self.groups
        self.part = self.half // 2

    def columns(self, slot, width=1):
        head = jnp.int32(slot)
        for level in range(self.steps + 1):
            head = lax.bitwise_xor(head, place_bit(level) * (self.heads >> (level + 1)))
        return pl.ds(pl.multiple_of(head * HEAD_DIM, HEAD_DIM), width * HEAD_DIM)

    def mask(self, group):
        return sum(((group >> (self.steps - 1 - j)) & 1) << j for j in range(self.steps))

    def base(self, part, far):
        return far * self.half + part * self.part

    def side(self, far):
        half = lax.bitwise_xor(jnp.int32(far), place_bit(0)) * (self.half * HEAD_DIM)
        return pl.ds(pl.multiple_of(half, HEAD_DIM), self.half * HEAD_DIM)


def key_value_body(plan, k_ref, v_ref, *rest):
    *parts, bits_ref, k_out, v_out, sems = rest
    copies = {}
    for far in (1, 0):
        at = plan.side(far)
        copies[far] = [
            pltpu.make_async_copy(k_ref.at[:, at], k_out.at[:, at], sems.at[0, far]),
            pltpu.make_async_copy(v_ref.at[:, at], v_out.at[:, at], sems.at[1, far]),
        ]
        for copy in copies[far]:
            copy.start()
    for level in range(bits_ref.shape[0]):
        bits_ref[level] = jnp.full(bits_ref.shape[1:], place_bit(level).astype(F32), F32)
    for far in (1, 0):
        for copy in copies[far]:
            copy.wait()
        for part in (0, 1):
            out_ref = parts[2 * (1 - far) + part]
            for number in range(plan.part):
                at = plan.columns(plan.base(part, far) + number)
                out_ref[number] = dot(k_out[:, at], v_out[:, at], TN).astype(out_ref.dtype)


def inner_body(plan, base, q_ref, k_ref, v_ref, *rest):
    *_, probs_ref, inner_ref = rest
    mask = causal_mask()
    for number in range(plan.half):
        at = plan.columns(base + number)
        probs = jnp.where(mask, dot(q_ref[:, at], k_ref[:, at], NT), 0.0).astype(BF)
        probs_ref[number] = probs
        inner_ref[number] = dot(probs, v_ref[:, at], NN)


def norm_body(plan, base, q_ref, g_ref, inner_ref, state_ref, normed_ref, raw_ref, grad_ref):
    for number in range(plan.part):
        at = plan.columns(base + number)
        query = q_ref[:, at]
        unnormed = inner_ref[base % plan.half + number] + dot(query, state_ref[number], NN)
        inv = lax.rsqrt(jnp.mean(unnormed * unnormed, axis=-1, keepdims=True) + EPSILON)
        normed = unnormed * inv
        normed_ref[number] = normed.astype(BF)
        cot = g_ref[:, at].astype(F32)
        raw = (cot - normed * jnp.mean(cot * normed, axis=-1, keepdims=True)) * inv
        raw = raw.astype(BF)
        raw_ref[number] = raw
        grad_ref[number] = dot(query, raw, TN).astype(grad_ref.dtype)


def local_grads_body(plan, far, q_ref, k_ref, v_ref, probs_ref, *rest):
    first, second, rest = rest[:3], rest[3:6], rest[6:]
    *_, gk_ref, gv_ref, normed_out, gq_out, gq_buf, sems = rest
    mask = causal_mask()
    copies, held = [], {}
    for part, refs in enumerate((first, second)):
        for number in range(plan.part):
            slot = plan.base(part, far) + number
            held[slot] = [ref.at[number] for ref in refs]
    for slot, (normed_ref, _, _) in held.items():
        at, number = plan.columns(slot), slot % plan.half
        copies.append(pltpu.make_async_copy(normed_ref, normed_out.at[:, at], sems.at[0, number]))
        copies[-1].start()
    for slot, (_, raw_ref, state_ref) in held.items():
        at, number = plan.columns(slot), slot % plan.half
        raw, state = raw_ref[...], state_ref[...]
        grad_probs = jnp.where(mask, dot(raw, v_ref[:, at], NT), 0.0).astype(BF)
        gq_buf[number] = (dot(grad_probs, k_ref[:, at], NN) + dot(raw, state, NT)).astype(BF)
        copies.append(pltpu.make_async_copy(gq_buf.at[number], gq_out.at[:, at], sems.at[1, number]))
        copies[-1].start()
        gk_ref[number] = dot(grad_probs, q_ref[:, at], TN)
        gv_ref[number] = dot(probs_ref[number], raw, TN)
    for copy in copies:
        copy.wait()


def last_grads_body(plan, pieces, k_ref, v_ref, gk_ref, gv_ref, *rest):
    states = rest[: len(pieces)]
    *_, gk_out, gv_out, gk_buf, gv_buf, sems = rest
    copies = []
    for (part, far), state_ref in zip(pieces, states):
        for inside in range(plan.part):
            slot = plan.base(part, far) + inside
            at, number = plan.columns(slot), slot % plan.half
            state = state_ref[inside]
            gk_buf[number] = (gk_ref[number] + dot(v_ref[:, at], state, NT)).astype(BF)
            copies.append(
                pltpu.make_async_copy(gk_buf.at[number], gk_out.at[:, at], sems.at[0, number])
            )
            copies[-1].start()
            gv_buf[number] = (gv_ref[number] + dot(k_ref[:, at], state, NN)).astype(BF)
            copies.append(
                pltpu.make_async_copy(gv_buf.at[number], gv_out.at[:, at], sems.at[1, number])
            )
            copies[-1].start()
    for copy in copies:
        copy.wait()


def hbm(shape, dtype):
    return jax.ShapeDtypeStruct(shape, dtype)


def call(body, arrays, outs, flops, scratch=(), raw_in=False, partial=()):
    if raw_in:
        arrays = [pltpu.with_memory_space_constraint(a, pltpu.HBM) for a in arrays]
    vmem, anywhere = pl.BlockSpec(memory_space=pltpu.VMEM), pl.BlockSpec(memory_space=pl.ANY)
    operands = [*arrays, *partial]
    in_specs = [pl.BlockSpec(memory_space=pltpu.HBM) if raw_in else vmem] * len(arrays) + [anywhere] * len(partial)
    whole = [isinstance(out, jax.ShapeDtypeStruct) for out in outs]
    first = whole.index(True) if True in whole else 0
    aliases = {len(arrays) + i: first + i for i in range(len(partial))}
    size = sum(a.size * a.dtype.itemsize for a in arrays) * 2
    return pl.pallas_call(
        body,
        out_shape=outs,
        in_specs=in_specs,
        out_specs=[anywhere if w else vmem for w in whole],
        scratch_shapes=list(scratch),
        input_output_aliases=aliases,
        compiler_params=pltpu.CompilerParams(vmem_limit_bytes=8 * 1024 * 1024),
        cost_estimate=pl.CostEstimate(flops=flops, bytes_accessed=size, transcendentals=0),
    )(*operands)


def swap(value, axes, mask):
    pairs = [(i, i ^ mask) for i in range(lax.axis_size(axes))]
    return lax.ppermute(value, axes, pairs)


def gated(value, bits, level, wanted):
    return jnp.where(bits[level, :1][None] == wanted, value, 0.0)


def before(own, others, target, bits, reverse):
    total = None
    for mask, state in ((0, own), *others.items()):
        if mask != target:
            step = (mask ^ target).bit_length() - 1
            wanted = 1.0 - ((target >> step) & 1)
            term = gated(state, bits, step + 1, 1.0 - wanted if reverse else wanted)
            total = term if total is None else total + term
    return total


def scan_states(plan, sends, keeps, bits, reverse, asides):
    chips = ("seq", "head")
    upper, lower = (0.0, 1.0) if reverse else (1.0, 0.0)
    given = {}

    def beside(name, value, axes, mask):
        if name not in asides:
            return swap(value, axes, mask)
        work, operands = asides[name]
        value, operands = lax.optimization_barrier((value, operands))
        got, given[name] = lax.optimization_barrier((swap(value, axes, mask), work(operands)))
        return got

    share = plan.groups // 2
    members = [range(share), range(share, plan.groups)]
    own, near_got, pair = {}, {}, {}
    for part, (send, keep) in enumerate(zip(sends, keeps)):
        got = swap(send, "sub", 1)
        for number, group in enumerate(members[part]):
            rows = slice(number * plan.kept, (number + 1) * plan.kept)
            own[group], near_got[group] = keep[rows], got[rows].astype(F32)
            pair[group] = own[group] + near_got[group]
    order = [group for part in members for group in part if group]
    others = {}
    for group in order:
        name = "share" if group == order[-1] else ""
        got = beside(name, pair[group].astype(BF), chips, plan.mask(group))
        others[plan.mask(group)] = got.astype(F32)
    total = pair[0]
    for state in others.values():
        total = total + state
    carried = jnp.zeros_like(total)
    for level in range(plan.steps, bits_in(chips)):
        name = "total" if level == bits_in(chips) - 1 else ""
        got = beside(name, total.astype(BF), chips, 1 << level).astype(F32)
        carried = carried + gated(got, bits, level + 1, upper)
        total = total + got
    sums = {0: carried + before(pair[0], others, 0, bits, reverse)}
    for group in order:
        message = carried + before(pair[0], others, plan.mask(group), bits, reverse)
        sums[group] = swap(message.astype(BF), chips, plan.mask(group)).astype(F32)
    near, far, message = [], [], None
    for part in members:
        if message is not None:
            for group in part:
                sums[group], message = lax.optimization_barrier((sums[group], message))
            far.append(swap(message, "sub", 1))
        message = [sums[group] + gated(own[group], bits, 0, lower) for group in part]
        known = [sums[group] + gated(near_got[group], bits, 0, upper) for group in part]
        message = jnp.concatenate(message).astype(BF)
        near.append(jnp.concatenate(known).astype(BF))
    far.append(swap(message, "sub", 1))
    return near, far, given


def on_device(query, key, value, cot):
    rows, width = query.shape
    plan = Plan(width // HEAD_DIM)
    levels = bits_in(AXES)
    part_state = (plan.part, HEAD_DIM, HEAD_DIM)
    half_state = (plan.half, HEAD_DIM, HEAD_DIM)
    unit = 2 * BLOCK * HEAD_DIM * HEAD_DIM * plan.half
    vm, dma = pltpu.VMEM, pltpu.SemaphoreType.DMA
    whole = hbm((rows, width), BF)

    *states, bits, key_vm, value_vm = call(
        functools.partial(key_value_body, plan), (key, value),
        [vm(part_state, BF)] * 2 + [vm(part_state, F32)] * 2
        + [vm((levels, 8, HEAD_DIM), F32), vm((rows, width), BF), vm((rows, width), BF)],
        unit * 2, (dma((2, 2)),), raw_in=True,
    )

    def inner_work(far, operands):
        return call(
            functools.partial(inner_body, plan, far * plan.half), operands,
            [vm(half_state, BF), vm(half_state, F32)], 2 * unit,
        )

    near, far, given = scan_states(
        plan, states[:2], states[2:], bits, False,
        {
            "share": (functools.partial(inner_work, 0), (query, key_vm, value_vm, cot)),
            "total": (functools.partial(inner_work, 1), (query, key_vm, value_vm)),
        },
    )
    inner = [given["share"], given["total"]]

    def norm(part, is_far, state):
        return call(
            functools.partial(norm_body, plan, plan.base(part, is_far)),
            (query, cot, inner[is_far][1], state),
            [vm(part_state, BF), vm(part_state, BF), vm(part_state, BF if is_far else F32)], unit,
        )

    normed = [[], []]
    for part in range(2):
        normed[0].append(norm(part, 0, near[part]))
        far[part], normed[0][part] = lax.optimization_barrier((far[part], normed[0][part]))
    for part in range(2):
        normed[1].append(norm(part, 1, far[part]))
    partials = ()

    def local_grads(is_far, operands):
        nonlocal partials
        out = call(
            functools.partial(local_grads_body, plan, is_far), operands,
            [vm(half_state, F32), vm(half_state, F32), whole, whole],
            5 * unit, (vm(half_state, BF), dma((2, plan.half))), partial=partials,
        )
        partials = out[2:]
        return out[:2]

    def operands(is_far, found):
        parts = [a for part in range(2) for a in (*normed[is_far][part][:2], found[part])]
        return (query, key_vm, value_vm, inner[is_far][0], *parts)

    near, far, given = scan_states(
        plan, [n[2] for n in normed[1]], [n[2] for n in normed[0]], bits, True,
        {
            "share": (functools.partial(local_grads, 0), operands(0, near)),
            "total": (functools.partial(local_grads, 1), operands(1, far)),
        },
    )
    grads = [given["share"], given["total"]]
    normed_out, grad_q = partials
    partials = ()
    buf = vm(half_state, BF)
    for pieces in (((0, 0), (1, 0)), ((0, 1), (1, 1))):
        is_far = pieces[0][1]
        found = [(far if is_far else near)[part] for part, _ in pieces]
        partials = call(
            functools.partial(last_grads_body, plan, pieces), (key_vm, value_vm, *grads[is_far], *found),
            [whole, whole], unit * len(pieces), (buf, buf, dma((2, plan.half))), partial=partials,
        )
        if not is_far:
            far, partials = lax.optimization_barrier((far, partials))
    grad_k, grad_v = partials
    return normed_out, grad_q, grad_k, grad_v


def solution(mesh):
    placed = P(("group", "seq", "head", "sub"), None)
    return jax.shard_map(
        on_device,
        mesh=mesh,
        in_specs=(placed,) * 4,
        out_specs=(placed,) * 4,
        check_vma=False,
    )
```

```python
import functools

import jax
import jax.numpy as jnp
from jax import lax
from jax.experimental import pallas as pl
from jax.experimental.pallas import tpu as pltpu
from jax.sharding import PartitionSpec as P

HEAD_DIM = 128
BLOCK = 128
EPSILON = 1e-05
BF = jnp.bfloat16
F32 = jnp.float32
NN = (((1,), (0,)), ((), ()))
NT = (((1,), (1,)), ((), ()))
TN = (((0,), (0,)), ((), ()))
AXES = ("seq", "head", "sub")


def dot(left, right, form):
    return lax.dot_general(left, right, form, preferred_element_type=F32)


def causal_mask():
    rows = lax.broadcasted_iota(jnp.int32, (BLOCK, BLOCK), 0)
    cols = lax.broadcasted_iota(jnp.int32, (BLOCK, BLOCK), 1)
    return rows >= cols


def place_bit(level):
    place = lax.axis_index(AXES).astype(jnp.int32)
    return lax.bitwise_and(lax.shift_right_logical(place, jnp.int32(level)), jnp.int32(1))


def bits_in(axis):
    return lax.axis_size(axis).bit_length() - 1


class Plan:
    def __init__(self, heads):
        self.heads, self.half = heads, heads // 2
        self.steps = bits_in("head") + (bits_in("seq") > 0)
        self.groups = 1 << self.steps
        self.kept = self.half // self.groups
        self.part = self.half // 2

    def head(self, slot, levels):
        head = jnp.int32(slot)
        for level in levels:
            head = lax.bitwise_xor(head, place_bit(level) * (self.heads >> (level + 1)))
        return head

    def columns(self, slot):
        head = self.head(slot, range(self.steps + 1))
        return pl.ds(pl.multiple_of(head * HEAD_DIM, HEAD_DIM), HEAD_DIM)

    def block(self, part, far):
        head = self.head(self.base(part, far), range(2))
        return pl.ds(pl.multiple_of(head * HEAD_DIM, HEAD_DIM), self.part * HEAD_DIM)

    def inside(self, number):
        head = self.head(number, range(2, self.steps + 1))
        return pl.ds(pl.multiple_of(head * HEAD_DIM, HEAD_DIM), HEAD_DIM)

    def mask(self, group):
        return sum(((group >> (self.steps - 1 - j)) & 1) << j for j in range(self.steps))

    def base(self, part, far):
        return far * self.half + part * self.part

    def side(self, far):
        half = lax.bitwise_xor(jnp.int32(far), place_bit(0)) * (self.half * HEAD_DIM)
        return pl.ds(pl.multiple_of(half, HEAD_DIM), self.half * HEAD_DIM)


def key_value_body(plan, k_ref, v_ref, *rest):
    *parts, bits_ref, k_out, v_out, sems = rest
    copies = {}
    for far in (1, 0):
        at = plan.side(far)
        copies[far] = [
            pltpu.make_async_copy(k_ref.at[:, at], k_out.at[:, at], sems.at[0, far]),
            pltpu.make_async_copy(v_ref.at[:, at], v_out.at[:, at], sems.at[1, far]),
        ]
        for copy in copies[far]:
            copy.start()
    for level in range(bits_ref.shape[0]):
        bits_ref[level] = jnp.full(bits_ref.shape[1:], place_bit(level).astype(F32), F32)
    for far in (1, 0):
        for copy in copies[far]:
            copy.wait()
        for part in (0, 1):
            out_ref = parts[2 * (1 - far) + part]
            for number in range(plan.part):
                at = plan.columns(plan.base(part, far) + number)
                out_ref[number] = dot(k_out[:, at], v_out[:, at], TN).astype(out_ref.dtype)


def inner_body(plan, base, q_ref, k_ref, v_ref, *rest):
    *_, probs_ref, inner_ref = rest
    mask = causal_mask()
    for number in range(plan.half):
        at = plan.columns(base + number)
        probs = jnp.where(mask, dot(q_ref[:, at], k_ref[:, at], NT), 0.0).astype(BF)
        probs_ref[number] = probs
        inner_ref[number] = dot(probs, v_ref[:, at], NN)


def norm_body(plan, base, q_ref, g_ref, inner_ref, state_ref, normed_ref, raw_ref, grad_ref):
    for number in range(plan.part):
        at = plan.columns(base + number)
        query = q_ref[:, at]
        unnormed = inner_ref[base % plan.half + number] + dot(query, state_ref[number], NN)
        inv = lax.rsqrt(jnp.mean(unnormed * unnormed, axis=-1, keepdims=True) + EPSILON)
        normed = unnormed * inv
        normed_ref[number] = normed.astype(BF)
        cot = g_ref[:, at].astype(F32)
        raw = (cot - normed * jnp.mean(cot * normed, axis=-1, keepdims=True)) * inv
        raw = raw.astype(BF)
        raw_ref[number] = raw
        grad_ref[number] = dot(query, raw, TN).astype(grad_ref.dtype)


def local_grads_body(plan, far, q_ref, k_ref, v_ref, probs_ref, *rest):
    found, rest = (rest[:3], rest[3:6]), rest[6:]
    *_, gk_ref, gv_ref, normed_out, gq_out, normed_buf, gq_buf, sems = rest
    mask = causal_mask()
    copies = []
    for part, (normed_ref, raw_ref, state_ref) in enumerate(found):
        for number in range(plan.part):
            normed_buf[part, :, plan.inside(number)] = normed_ref[number]
        to = plan.block(part, far)
        copies.append(pltpu.make_async_copy(normed_buf.at[part], normed_out.at[:, to], sems.at[0, part]))
        copies[-1].start()
    for part, (normed_ref, raw_ref, state_ref) in enumerate(found):
        for number in range(plan.part):
            slot = part * plan.part + number
            at = plan.columns(far * plan.half + slot)
            raw, state = raw_ref[number], state_ref[number]
            grad_probs = jnp.where(mask, dot(raw, v_ref[:, at], NT), 0.0).astype(BF)
            grad_query = dot(grad_probs, k_ref[:, at], NN) + dot(raw, state, NT)
            gq_buf[part, :, plan.inside(number)] = grad_query.astype(BF)
            gk_ref[slot] = dot(grad_probs, q_ref[:, at], TN)
            gv_ref[slot] = dot(probs_ref[slot], raw, TN)
        to = plan.block(part, far)
        copies.append(pltpu.make_async_copy(gq_buf.at[part], gq_out.at[:, to], sems.at[1, part]))
        copies[-1].start()
    for copy in copies:
        copy.wait()


def last_grads(plan, part, far, k_ref, v_ref, gk_ref, gv_ref, state_ref, gk_to, gv_to):
    for number in range(plan.part):
        slot = part * plan.part + number
        at, to = plan.columns(far * plan.half + slot), plan.inside(number)
        state = state_ref[number]
        gk_to[part, :, to] = (gk_ref[slot] + dot(v_ref[:, at], state, NT)).astype(BF)
        gv_to[part, :, to] = (gv_ref[slot] + dot(k_ref[:, at], state, NN)).astype(BF)


def near_grads_body(plan, k_ref, v_ref, gk_ref, gv_ref, *rest):
    *states, gk_out, gv_out = rest
    for part, state_ref in enumerate(states):
        last_grads(plan, part, 0, k_ref, v_ref, gk_ref, gv_ref, state_ref, gk_out, gv_out)


def far_grads_body(plan, k_ref, v_ref, gk_ref, gv_ref, *rest):
    *states, gk_near, gv_near, gk_out, gv_out, gk_buf, gv_buf, sems = rest
    copies = []

    def leave(part, far, pair):
        to = plan.block(part, far)
        for number, (ref, out) in enumerate(zip(pair, (gk_out, gv_out))):
            sem = sems.at[number, far, part]
            copies.append(pltpu.make_async_copy(ref.at[part], out.at[:, to], sem))
            copies[-1].start()

    for part in range(2):
        leave(part, 0, (gk_near, gv_near))
    for part, state_ref in enumerate(states):
        last_grads(plan, part, 1, k_ref, v_ref, gk_ref, gv_ref, state_ref, gk_buf, gv_buf)
        leave(part, 1, (gk_buf, gv_buf))
    for copy in copies:
        copy.wait()


def hbm(shape, dtype):
    return jax.ShapeDtypeStruct(shape, dtype)


def call(body, arrays, outs, flops, scratch=(), raw_in=False, partial=()):
    if raw_in:
        arrays = [pltpu.with_memory_space_constraint(a, pltpu.HBM) for a in arrays]
    vmem, anywhere = pl.BlockSpec(memory_space=pltpu.VMEM), pl.BlockSpec(memory_space=pl.ANY)
    operands = [*arrays, *partial]
    in_specs = [pl.BlockSpec(memory_space=pltpu.HBM) if raw_in else vmem] * len(arrays) + [anywhere] * len(partial)
    whole = [isinstance(out, jax.ShapeDtypeStruct) for out in outs]
    first = whole.index(True) if True in whole else 0
    aliases = {len(arrays) + i: first + i for i in range(len(partial))}
    size = sum(a.size * a.dtype.itemsize for a in arrays) * 2
    return pl.pallas_call(
        body,
        out_shape=outs,
        in_specs=in_specs,
        out_specs=[anywhere if w else vmem for w in whole],
        scratch_shapes=list(scratch),
        input_output_aliases=aliases,
        compiler_params=pltpu.CompilerParams(vmem_limit_bytes=8 * 1024 * 1024),
        cost_estimate=pl.CostEstimate(flops=flops, bytes_accessed=size, transcendentals=0),
    )(*operands)


def swap(value, axes, mask):
    pairs = [(i, i ^ mask) for i in range(lax.axis_size(axes))]
    return lax.ppermute(value, axes, pairs)


def gated(value, bits, level, wanted):
    return jnp.where(bits[level, :1][None] == wanted, value, 0.0)


def before(own, others, target, bits, reverse):
    total = None
    for mask, state in ((0, own), *others.items()):
        if mask != target:
            step = (mask ^ target).bit_length() - 1
            wanted = 1.0 - ((target >> step) & 1)
            term = gated(state, bits, step + 1, 1.0 - wanted if reverse else wanted)
            total = term if total is None else total + term
    return total


def scan_states(plan, sends, keeps, bits, reverse, asides):
    chips = ("seq", "head")
    upper, lower = (0.0, 1.0) if reverse else (1.0, 0.0)
    given = {}

    def beside(name, value, axes, mask):
        if name not in asides:
            return swap(value, axes, mask)
        work, operands = asides[name]
        value, operands = lax.optimization_barrier((value, operands))
        got, given[name] = lax.optimization_barrier((swap(value, axes, mask), work(operands)))
        return got

    share = plan.groups // 2
    members = [range(share), range(share, plan.groups)]
    own, near_got, pair = {}, {}, {}
    for part, (send, keep) in enumerate(zip(sends, keeps)):
        got = swap(send, "sub", 1)
        for number, group in enumerate(members[part]):
            rows = slice(number * plan.kept, (number + 1) * plan.kept)
            own[group], near_got[group] = keep[rows], got[rows].astype(F32)
            pair[group] = own[group] + near_got[group]
    order = [group for part in members for group in part if group]
    others = {}
    for group in order:
        name = "share" if group == order[-1] else ""
        got = beside(name, pair[group].astype(BF), chips, plan.mask(group))
        others[plan.mask(group)] = got.astype(F32)
    total = pair[0]
    for state in others.values():
        total = total + state
    carried = jnp.zeros_like(total)
    for level in range(plan.steps, bits_in(chips)):
        name = "total" if level == bits_in(chips) - 1 else ""
        got = beside(name, total.astype(BF), chips, 1 << level).astype(F32)
        carried = carried + gated(got, bits, level + 1, upper)
        total = total + got
    sums = {0: carried + before(pair[0], others, 0, bits, reverse)}
    for group in order:
        message = carried + before(pair[0], others, plan.mask(group), bits, reverse)
        sums[group] = swap(message.astype(BF), chips, plan.mask(group)).astype(F32)
    near, far, message = [], [], None
    for part in members:
        if message is not None:
            for group in part:
                sums[group], message = lax.optimization_barrier((sums[group], message))
            far.append(swap(message, "sub", 1))
        message = [sums[group] + gated(own[group], bits, 0, lower) for group in part]
        known = [sums[group] + gated(near_got[group], bits, 0, upper) for group in part]
        message = jnp.concatenate(message).astype(BF)
        near.append(jnp.concatenate(known).astype(BF))
    far.append(swap(message, "sub", 1))
    return near, far, given


def on_device(query, key, value, cot):
    rows, width = query.shape
    plan = Plan(width // HEAD_DIM)
    levels = bits_in(AXES)
    part_state = (plan.part, HEAD_DIM, HEAD_DIM)
    half_state = (plan.half, HEAD_DIM, HEAD_DIM)
    unit = 2 * BLOCK * HEAD_DIM * HEAD_DIM * plan.half
    vm, dma = pltpu.VMEM, pltpu.SemaphoreType.DMA
    whole = hbm((rows, width), BF)
    buf = vm((2, rows, plan.part * HEAD_DIM), BF)

    *states, bits, key_vm, value_vm = call(
        functools.partial(key_value_body, plan), (key, value),
        [vm(part_state, BF)] * 2 + [vm(part_state, F32)] * 2
        + [vm((levels, 8, HEAD_DIM), F32), vm((rows, width), BF), vm((rows, width), BF)],
        unit * 2, (dma((2, 2)),), raw_in=True,
    )

    def inner_work(far, operands):
        return call(
            functools.partial(inner_body, plan, far * plan.half), operands,
            [vm(half_state, BF), vm(half_state, F32)], 2 * unit,
        )

    near, far, given = scan_states(
        plan, states[:2], states[2:], bits, False,
        {
            "share": (functools.partial(inner_work, 0), (query, key_vm, value_vm, cot)),
            "total": (functools.partial(inner_work, 1), (query, key_vm, value_vm)),
        },
    )
    inner = [given["share"], given["total"]]

    def norm(part, is_far, state):
        return call(
            functools.partial(norm_body, plan, plan.base(part, is_far)),
            (query, cot, inner[is_far][1], state),
            [vm(part_state, BF), vm(part_state, BF), vm(part_state, BF if is_far else F32)], unit,
        )

    normed = [[None, None], []]
    normed[0][0] = norm(0, 0, near[0])
    far[0], normed[0][0] = lax.optimization_barrier((far[0], normed[0][0]))
    for part in range(2):
        normed[1].append(norm(part, 1, far[part]))
    near[1], normed[1] = lax.optimization_barrier((near[1], normed[1]))
    normed[0][1] = norm(1, 0, near[1])
    partials = ()

    def local_grads(is_far, operands):
        nonlocal partials
        out = call(
            functools.partial(local_grads_body, plan, is_far), operands,
            [vm(half_state, F32), vm(half_state, F32), whole, whole],
            5 * unit, (buf, buf, dma((2, 2))), partial=partials,
        )
        partials = out[2:]
        return out[:2]

    def operands(is_far, found):
        parts = [a for part in range(2) for a in (*normed[is_far][part][:2], found[part])]
        return (query, key_vm, value_vm, inner[is_far][0], *parts)

    near, far, given = scan_states(
        plan, [n[2] for n in normed[1]], [n[2] for n in normed[0]], bits, True,
        {
            "share": (functools.partial(local_grads, 0), operands(0, near)),
            "total": (functools.partial(local_grads, 1), operands(1, far)),
        },
    )
    grads = [given["share"], given["total"]]
    normed_out, grad_q = partials
    near_grads = call(
        functools.partial(near_grads_body, plan), (key_vm, value_vm, *grads[0], *near),
        [buf, buf], 2 * unit,
    )
    far, near_grads = lax.optimization_barrier((far, near_grads))
    grad_k, grad_v = call(
        functools.partial(far_grads_body, plan), (key_vm, value_vm, *grads[1], *far, *near_grads),
        [whole, whole], 2 * unit, (buf, buf, dma((2, 2, 2))),
    )
    return normed_out, grad_q, grad_k, grad_v


def solution(mesh):
    placed = P(("group", "seq", "head", "sub"), None)
    return jax.shard_map(
        on_device,
        mesh=mesh,
        in_specs=(placed,) * 4,
        out_specs=(placed,) * 4,
        check_vma=False,
    )
```

```python
import functools

import jax
import jax.numpy as jnp
from jax import lax
from jax.experimental import pallas as pl
from jax.experimental.pallas import tpu as pltpu
from jax.sharding import PartitionSpec as P

HEAD_DIM = 128
BLOCK = 128
EPSILON = 1e-05
BF = jnp.bfloat16
F32 = jnp.float32
NN = (((1,), (0,)), ((), ()))
NT = (((1,), (1,)), ((), ()))
TN = (((0,), (0,)), ((), ()))
AXES = ("seq", "head", "sub")
BACK = (1, 0)


def dot(left, right, form):
    return lax.dot_general(left, right, form, preferred_element_type=F32)


def causal_mask():
    rows = lax.broadcasted_iota(jnp.int32, (BLOCK, BLOCK), 0)
    cols = lax.broadcasted_iota(jnp.int32, (BLOCK, BLOCK), 1)
    return rows >= cols


def place_bit(level):
    place = lax.axis_index(AXES).astype(jnp.int32)
    return lax.bitwise_and(lax.shift_right_logical(place, jnp.int32(level)), jnp.int32(1))


def bits_in(axis):
    return lax.axis_size(axis).bit_length() - 1


class Plan:
    def __init__(self, heads):
        self.heads, self.half = heads, heads // 2
        self.steps = bits_in("head") + (bits_in("seq") > 0)
        self.groups = 1 << self.steps
        self.kept = self.half // self.groups
        self.part = self.half // 2

    def head(self, slot, levels):
        head = jnp.int32(slot)
        for level in levels:
            head = lax.bitwise_xor(head, place_bit(level) * (self.heads >> (level + 1)))
        return head

    def columns(self, slot):
        head = self.head(slot, range(self.steps + 1))
        return pl.ds(pl.multiple_of(head * HEAD_DIM, HEAD_DIM), HEAD_DIM)

    def block(self, part, far):
        head = self.head(self.base(part, far), range(2))
        return pl.ds(pl.multiple_of(head * HEAD_DIM, HEAD_DIM), self.part * HEAD_DIM)

    def inside(self, number):
        head = self.head(number, range(2, self.steps + 1))
        return pl.ds(pl.multiple_of(head * HEAD_DIM, HEAD_DIM), HEAD_DIM)

    def mask(self, group):
        return sum(((group >> (self.steps - 1 - j)) & 1) << j for j in range(self.steps))

    def base(self, part, far):
        return far * self.half + part * self.part

    def side(self, far):
        half = lax.bitwise_xor(jnp.int32(far), place_bit(0)) * (self.half * HEAD_DIM)
        return pl.ds(pl.multiple_of(half, HEAD_DIM), self.half * HEAD_DIM)


def key_value_body(plan, k_ref, v_ref, *rest):
    *parts, bits_ref, k_out, v_out, sems = rest
    copies = {}
    for far in (1, 0):
        at = plan.side(far)
        copies[far] = [
            pltpu.make_async_copy(k_ref.at[:, at], k_out.at[:, at], sems.at[0, far]),
            pltpu.make_async_copy(v_ref.at[:, at], v_out.at[:, at], sems.at[1, far]),
        ]
        for copy in copies[far]:
            copy.start()
    for level in range(bits_ref.shape[0]):
        bits_ref[level] = jnp.full(bits_ref.shape[1:], place_bit(level).astype(F32), F32)
    for far in (1, 0):
        for copy in copies[far]:
            copy.wait()
        for part in (0, 1):
            out_ref = parts[2 * (1 - far) + part]
            for number in range(plan.part):
                at = plan.columns(plan.base(part, far) + number)
                out_ref[number] = dot(k_out[:, at], v_out[:, at], TN).astype(out_ref.dtype)


def inner_body(plan, base, q_ref, k_ref, v_ref, *rest):
    *_, probs_ref, inner_ref = rest
    mask = causal_mask()
    for number in range(plan.half):
        at = plan.columns(base + number)
        probs = jnp.where(mask, dot(q_ref[:, at], k_ref[:, at], NT), 0.0).astype(BF)
        probs_ref[number] = probs
        inner_ref[number] = dot(probs, v_ref[:, at], NN)


def norm_body(plan, base, q_ref, g_ref, inner_ref, state_ref, normed_ref, raw_ref, grad_ref):
    for number in range(plan.part):
        at = plan.columns(base + number)
        query = q_ref[:, at]
        unnormed = inner_ref[base % plan.half + number] + dot(query, state_ref[number], NN)
        inv = lax.rsqrt(jnp.mean(unnormed * unnormed, axis=-1, keepdims=True) + EPSILON)
        normed = unnormed * inv
        normed_ref[number] = normed.astype(BF)
        cot = g_ref[:, at].astype(F32)
        raw = (cot - normed * jnp.mean(cot * normed, axis=-1, keepdims=True)) * inv
        raw = raw.astype(BF)
        raw_ref[number] = raw
        grad_ref[number] = dot(query, raw, TN).astype(grad_ref.dtype)


def local_grads_body(plan, far, q_ref, k_ref, v_ref, probs_ref, *rest):
    found, rest = (rest[:3], rest[3:6]), rest[6:]
    *_, gk_ref, gv_ref, normed_out, gq_out, normed_buf, gq_buf, sems = rest
    mask = causal_mask()
    copies = []
    for part, (normed_ref, raw_ref, state_ref) in enumerate(found):
        for number in range(plan.part):
            normed_buf[part, :, plan.inside(number)] = normed_ref[number]
        to = plan.block(part, far)
        copies.append(pltpu.make_async_copy(normed_buf.at[part], normed_out.at[:, to], sems.at[0, part]))
        copies[-1].start()
    for part, (normed_ref, raw_ref, state_ref) in enumerate(found):
        for number in range(plan.part):
            slot = part * plan.part + number
            at = plan.columns(far * plan.half + slot)
            raw, state = raw_ref[number], state_ref[number]
            grad_probs = jnp.where(mask, dot(raw, v_ref[:, at], NT), 0.0).astype(BF)
            grad_query = dot(grad_probs, k_ref[:, at], NN) + dot(raw, state, NT)
            gq_buf[part, :, plan.inside(number)] = grad_query.astype(BF)
            gk_ref[slot] = dot(grad_probs, q_ref[:, at], TN)
            gv_ref[slot] = dot(probs_ref[slot], raw, TN)
        to = plan.block(part, far)
        copies.append(pltpu.make_async_copy(gq_buf.at[part], gq_out.at[:, to], sems.at[1, part]))
        copies[-1].start()
    for copy in copies:
        copy.wait()


def last_grads(plan, part, far, k_ref, v_ref, gk_ref, gv_ref, state_ref, gk_to, gv_to):
    for number in range(plan.part):
        slot = part * plan.part + number
        at, to = plan.columns(far * plan.half + slot), plan.inside(number)
        state = state_ref[number]
        gk_to[part, :, to] = (gk_ref[slot] + dot(v_ref[:, at], state, NT)).astype(BF)
        gv_to[part, :, to] = (gv_ref[slot] + dot(k_ref[:, at], state, NN)).astype(BF)


def near_grads_body(plan, k_ref, v_ref, gk_ref, gv_ref, *rest):
    *states, gk_out, gv_out = rest
    for part, state_ref in enumerate(states):
        last_grads(plan, part, 0, k_ref, v_ref, gk_ref, gv_ref, state_ref, gk_out, gv_out)


def far_grads_body(plan, k_ref, v_ref, gk_ref, gv_ref, *rest):
    *states, gk_near, gv_near, gk_out, gv_out, gk_buf, gv_buf, sems = rest
    copies = []

    def leave(part, far, pair):
        to = plan.block(part, far)
        for number, (ref, out) in enumerate(zip(pair, (gk_out, gv_out))):
            sem = sems.at[number, far, part]
            copies.append(pltpu.make_async_copy(ref.at[part], out.at[:, to], sem))
            copies[-1].start()

    for part in range(2):
        leave(part, 0, (gk_near, gv_near))
    for part, state_ref in enumerate(states):
        last_grads(plan, part, 1, k_ref, v_ref, gk_ref, gv_ref, state_ref, gk_buf, gv_buf)
        leave(part, 1, (gk_buf, gv_buf))
    for copy in copies:
        copy.wait()


def hbm(shape, dtype):
    return jax.ShapeDtypeStruct(shape, dtype)


def call(body, arrays, outs, flops, scratch=(), raw_in=False, partial=()):
    if raw_in:
        arrays = [pltpu.with_memory_space_constraint(a, pltpu.HBM) for a in arrays]
    vmem, anywhere = pl.BlockSpec(memory_space=pltpu.VMEM), pl.BlockSpec(memory_space=pl.ANY)
    operands = [*arrays, *partial]
    in_specs = [pl.BlockSpec(memory_space=pltpu.HBM) if raw_in else vmem] * len(arrays) + [anywhere] * len(partial)
    whole = [isinstance(out, jax.ShapeDtypeStruct) for out in outs]
    first = whole.index(True) if True in whole else 0
    aliases = {len(arrays) + i: first + i for i in range(len(partial))}
    size = sum(a.size * a.dtype.itemsize for a in arrays) * 2
    return pl.pallas_call(
        body,
        out_shape=outs,
        in_specs=in_specs,
        out_specs=[anywhere if w else vmem for w in whole],
        scratch_shapes=list(scratch),
        input_output_aliases=aliases,
        compiler_params=pltpu.CompilerParams(vmem_limit_bytes=8 * 1024 * 1024),
        cost_estimate=pl.CostEstimate(flops=flops, bytes_accessed=size, transcendentals=0),
    )(*operands)


def swap(value, axes, mask):
    pairs = [(i, i ^ mask) for i in range(lax.axis_size(axes))]
    return lax.ppermute(value, axes, pairs)


def gated(value, bits, level, wanted):
    return jnp.where(bits[level, :1][None] == wanted, value, 0.0)


def before(own, others, target, bits, reverse):
    total = None
    for mask, state in ((0, own), *others.items()):
        if mask != target:
            step = (mask ^ target).bit_length() - 1
            wanted = 1.0 - ((target >> step) & 1)
            term = gated(state, bits, step + 1, 1.0 - wanted if reverse else wanted)
            total = term if total is None else total + term
    return total


def scan_states(plan, sends, keeps, bits, reverse, asides):
    chips = ("seq", "head")
    upper, lower = (0.0, 1.0) if reverse else (1.0, 0.0)
    given = {}

    def beside(name, value, axes, mask):
        if name not in asides:
            return swap(value, axes, mask)
        work, operands = asides[name]
        value, operands = lax.optimization_barrier((value, operands))
        got, given[name] = lax.optimization_barrier((swap(value, axes, mask), work(operands)))
        return got

    share = plan.groups // 2
    members = [range(share), range(share, plan.groups)]
    own, near_got, pair = {}, {}, {}
    for part, (send, keep) in enumerate(zip(sends, keeps)):
        got = swap(send, "sub", 1)
        for number, group in enumerate(members[part]):
            rows = slice(number * plan.kept, (number + 1) * plan.kept)
            own[group], near_got[group] = keep[rows], got[rows].astype(F32)
            pair[group] = own[group] + near_got[group]
    order = [group for part in members for group in part if group]
    others = {}
    for group in order:
        name = "share" if group == order[-1] else ""
        got = beside(name, pair[group].astype(BF), chips, plan.mask(group))
        others[plan.mask(group)] = got.astype(F32)
    total = pair[0]
    for state in others.values():
        total = total + state
    carried = jnp.zeros_like(total)
    for level in range(plan.steps, bits_in(chips)):
        name = "total" if level == bits_in(chips) - 1 else ""
        got = beside(name, total.astype(BF), chips, 1 << level).astype(F32)
        carried = carried + gated(got, bits, level + 1, upper)
        total = total + got
    sums = {0: carried + before(pair[0], others, 0, bits, reverse)}
    for group in order:
        message = carried + before(pair[0], others, plan.mask(group), bits, reverse)
        sums[group] = swap(message.astype(BF), chips, plan.mask(group)).astype(F32)
    near, far, message = [None, None], [None, None], None
    for part in BACK:
        if message is not None:
            for group in members[part]:
                sums[group], message = lax.optimization_barrier((sums[group], message))
            far[1 - part] = swap(message, "sub", 1)
        message = [sums[group] + gated(own[group], bits, 0, lower) for group in members[part]]
        known = [sums[group] + gated(near_got[group], bits, 0, upper) for group in members[part]]
        message = jnp.concatenate(message).astype(BF)
        near[part] = jnp.concatenate(known).astype(BF)
    far[BACK[1]] = swap(message, "sub", 1)
    return near, far, given


def on_device(query, key, value, cot):
    rows, width = query.shape
    plan = Plan(width // HEAD_DIM)
    levels = bits_in(AXES)
    part_state = (plan.part, HEAD_DIM, HEAD_DIM)
    half_state = (plan.half, HEAD_DIM, HEAD_DIM)
    unit = 2 * BLOCK * HEAD_DIM * HEAD_DIM * plan.half
    vm, dma = pltpu.VMEM, pltpu.SemaphoreType.DMA
    whole = hbm((rows, width), BF)
    buf = vm((2, rows, plan.part * HEAD_DIM), BF)

    *states, bits, key_vm, value_vm = call(
        functools.partial(key_value_body, plan), (key, value),
        [vm(part_state, BF)] * 2 + [vm(part_state, F32)] * 2
        + [vm((levels, 8, HEAD_DIM), F32), vm((rows, width), BF), vm((rows, width), BF)],
        unit * 2, (dma((2, 2)),), raw_in=True,
    )

    def inner_work(far, operands):
        return call(
            functools.partial(inner_body, plan, far * plan.half), operands,
            [vm(half_state, BF), vm(half_state, F32)], 2 * unit,
        )

    near, far, given = scan_states(
        plan, states[:2], states[2:], bits, False,
        {
            "share": (functools.partial(inner_work, 0), (query, key_vm, value_vm, cot)),
            "total": (functools.partial(inner_work, 1), (query, key_vm, value_vm)),
        },
    )
    inner = [given["share"], given["total"]]

    def norm(part, is_far, state):
        return call(
            functools.partial(norm_body, plan, plan.base(part, is_far)),
            (query, cot, inner[is_far][1], state),
            [vm(part_state, BF), vm(part_state, BF), vm(part_state, BF if is_far else F32)], unit,
        )

    normed = [[None, None], [None, None]]
    early, late = BACK
    normed[0][early] = norm(early, 0, near[early])
    far[early], normed[0][early] = lax.optimization_barrier((far[early], normed[0][early]))
    for part in BACK:
        normed[1][part] = norm(part, 1, far[part])
    near[late], normed[1] = lax.optimization_barrier((near[late], normed[1]))
    normed[0][late] = norm(late, 0, near[late])
    partials = ()

    def local_grads(is_far, operands):
        nonlocal partials
        out = call(
            functools.partial(local_grads_body, plan, is_far), operands,
            [vm(half_state, F32), vm(half_state, F32), whole, whole],
            5 * unit, (buf, buf, dma((2, 2))), partial=partials,
        )
        partials = out[2:]
        return out[:2]

    def operands(is_far, found):
        parts = [a for part in range(2) for a in (*normed[is_far][part][:2], found[part])]
        return (query, key_vm, value_vm, inner[is_far][0], *parts)

    near, far, given = scan_states(
        plan, [n[2] for n in normed[1]], [n[2] for n in normed[0]], bits, True,
        {
            "share": (functools.partial(local_grads, 0), operands(0, near)),
            "total": (functools.partial(local_grads, 1), operands(1, far)),
        },
    )
    grads = [given["share"], given["total"]]
    normed_out, grad_q = partials
    near_grads = call(
        functools.partial(near_grads_body, plan), (key_vm, value_vm, *grads[0], *near),
        [buf, buf], 2 * unit,
    )
    far, near_grads = lax.optimization_barrier((far, near_grads))
    grad_k, grad_v = call(
        functools.partial(far_grads_body, plan), (key_vm, value_vm, *grads[1], *far, *near_grads),
        [whole, whole], 2 * unit, (buf, buf, dma((2, 2, 2))),
    )
    return normed_out, grad_q, grad_k, grad_v


def solution(mesh):
    placed = P(("group", "seq", "head", "sub"), None)
    return jax.shard_map(
        on_device,
        mesh=mesh,
        in_specs=(placed,) * 4,
        out_specs=(placed,) * 4,
        check_vma=False,
    )
```

```python
import functools

import jax
import jax.numpy as jnp
from jax import lax
from jax.experimental import pallas as pl
from jax.experimental.pallas import tpu as pltpu
from jax.sharding import PartitionSpec as P

HEAD_DIM = 128
BLOCK = 128
EPSILON = 1e-05
BF = jnp.bfloat16
F32 = jnp.float32
NN = (((1,), (0,)), ((), ()))
NT = (((1,), (1,)), ((), ()))
TN = (((0,), (0,)), ((), ()))
AXES = ("seq", "head", "sub")
BACK = (1, 0)


def dot(left, right, form):
    return lax.dot_general(left, right, form, preferred_element_type=F32)


def causal_mask():
    rows = lax.broadcasted_iota(jnp.int32, (BLOCK, BLOCK), 0)
    cols = lax.broadcasted_iota(jnp.int32, (BLOCK, BLOCK), 1)
    return rows >= cols


def place_bit(level):
    place = lax.axis_index(AXES).astype(jnp.int32)
    return lax.bitwise_and(lax.shift_right_logical(place, jnp.int32(level)), jnp.int32(1))


def bits_in(axis):
    return lax.axis_size(axis).bit_length() - 1


class Plan:
    def __init__(self, heads):
        self.heads, self.half = heads, heads // 2
        self.steps = bits_in("head") + (bits_in("seq") > 0)
        self.groups = 1 << self.steps
        self.kept = self.half // self.groups
        self.part = self.half // 2

    def head(self, slot, levels):
        head = jnp.int32(slot)
        for level in levels:
            head = lax.bitwise_xor(head, place_bit(level) * (self.heads >> (level + 1)))
        return head

    def columns(self, slot):
        head = self.head(slot, range(self.steps + 1))
        return pl.ds(pl.multiple_of(head * HEAD_DIM, HEAD_DIM), HEAD_DIM)

    def block(self, part, far):
        head = self.head(self.base(part, far), range(2))
        return pl.ds(pl.multiple_of(head * HEAD_DIM, HEAD_DIM), self.part * HEAD_DIM)

    def inside(self, number):
        head = self.head(number, range(2, self.steps + 1))
        return pl.ds(pl.multiple_of(head * HEAD_DIM, HEAD_DIM), HEAD_DIM)

    def mask(self, group):
        return sum(((group >> (self.steps - 1 - j)) & 1) << j for j in range(self.steps))

    def base(self, part, far):
        return far * self.half + part * self.part

    def side(self, far):
        half = lax.bitwise_xor(jnp.int32(far), place_bit(0)) * (self.half * HEAD_DIM)
        return pl.ds(pl.multiple_of(half, HEAD_DIM), self.half * HEAD_DIM)


def key_value_body(plan, k_ref, v_ref, *rest):
    *parts, bits_ref, k_out, v_out, sems = rest
    copies = {}
    for far in (1, 0):
        at = plan.side(far)
        copies[far] = [
            pltpu.make_async_copy(k_ref.at[:, at], k_out.at[:, at], sems.at[0, far]),
            pltpu.make_async_copy(v_ref.at[:, at], v_out.at[:, at], sems.at[1, far]),
        ]
        for copy in copies[far]:
            copy.start()
    for level in range(bits_ref.shape[0]):
        bits_ref[level] = jnp.full(bits_ref.shape[1:], place_bit(level).astype(F32), F32)
    for far in (1, 0):
        for copy in copies[far]:
            copy.wait()
        for part in (0, 1):
            out_ref = parts[2 * (1 - far) + part]
            for number in range(plan.part):
                at = plan.columns(plan.base(part, far) + number)
                out_ref[number] = dot(k_out[:, at], v_out[:, at], TN).astype(out_ref.dtype)


def inner_body(plan, base, q_ref, k_ref, v_ref, *rest):
    *_, probs_ref, inner_ref = rest
    mask = causal_mask()
    for number in range(plan.half):
        at = plan.columns(base + number)
        probs = jnp.where(mask, dot(q_ref[:, at], k_ref[:, at], NT), 0.0).astype(BF)
        probs_ref[number] = probs
        inner_ref[number] = dot(probs, v_ref[:, at], NN)


def norm_body(plan, base, q_ref, g_ref, inner_ref, state_ref, normed_ref, raw_ref, grad_ref):
    for number in range(plan.part):
        at = plan.columns(base + number)
        query = q_ref[:, at]
        unnormed = inner_ref[base % plan.half + number] + dot(query, state_ref[number], NN)
        inv = lax.rsqrt(jnp.mean(unnormed * unnormed, axis=-1, keepdims=True) + EPSILON)
        normed = unnormed * inv
        normed_ref[number] = normed.astype(BF)
        cot = g_ref[:, at].astype(F32)
        raw = (cot - normed * jnp.mean(cot * normed, axis=-1, keepdims=True)) * inv
        raw = raw.astype(BF)
        raw_ref[number] = raw
        grad_ref[number] = dot(query, raw, TN).astype(grad_ref.dtype)


def local_grads_body(plan, far, q_ref, k_ref, v_ref, probs_ref, *rest):
    found, rest = (rest[:3], rest[3:6]), rest[6:]
    *_, gk_ref, gv_ref, normed_out, gq_out, normed_buf, gq_buf, sems = rest
    mask = causal_mask()
    copies = []
    for part, (normed_ref, raw_ref, state_ref) in enumerate(found):
        for number in range(plan.part):
            normed_buf[part, :, plan.inside(number)] = normed_ref[number]
        to = plan.block(part, far)
        copies.append(pltpu.make_async_copy(normed_buf.at[part], normed_out.at[:, to], sems.at[0, part]))
        copies[-1].start()
    for part, (normed_ref, raw_ref, state_ref) in enumerate(found):
        for number in range(plan.part):
            slot = part * plan.part + number
            at = plan.columns(far * plan.half + slot)
            raw, state = raw_ref[number], state_ref[number]
            grad_probs = jnp.where(mask, dot(raw, v_ref[:, at], NT), 0.0).astype(BF)
            grad_query = dot(grad_probs, k_ref[:, at], NN) + dot(raw, state, NT)
            gq_buf[part, :, plan.inside(number)] = grad_query.astype(BF)
            gk_ref[slot] = dot(grad_probs, q_ref[:, at], TN)
            gv_ref[slot] = dot(probs_ref[slot], raw, TN)
        to = plan.block(part, far)
        copies.append(pltpu.make_async_copy(gq_buf.at[part], gq_out.at[:, to], sems.at[1, part]))
        copies[-1].start()
    for copy in copies:
        copy.wait()


def last_grads(plan, part, far, k_ref, v_ref, gk_ref, gv_ref, state_ref, gk_to, gv_to):
    for number in range(plan.part):
        slot = part * plan.part + number
        at, to = plan.columns(far * plan.half + slot), plan.inside(number)
        state = state_ref[number]
        gk_to[part, :, to] = (gk_ref[slot] + dot(v_ref[:, at], state, NT)).astype(BF)
        gv_to[part, :, to] = (gv_ref[slot] + dot(k_ref[:, at], state, NN)).astype(BF)


def near_grads_body(plan, k_ref, v_ref, gk_ref, gv_ref, *rest):
    *states, gk_out, gv_out = rest
    for part, state_ref in enumerate(states):
        last_grads(plan, part, 0, k_ref, v_ref, gk_ref, gv_ref, state_ref, gk_out, gv_out)


def far_grads_body(plan, k_ref, v_ref, gk_ref, gv_ref, *rest):
    *states, gk_near, gv_near, gk_out, gv_out, gk_buf, gv_buf, sems = rest
    copies = []

    def leave(part, far, pair):
        to = plan.block(part, far)
        for number, (ref, out) in enumerate(zip(pair, (gk_out, gv_out))):
            sem = sems.at[number, far, part]
            copies.append(pltpu.make_async_copy(ref.at[part], out.at[:, to], sem))
            copies[-1].start()

    for part in range(2):
        leave(part, 0, (gk_near, gv_near))
    for part in range(2):
        state_ref = states[0].at[pl.ds(part * plan.part, plan.part)]
        last_grads(plan, part, 1, k_ref, v_ref, gk_ref, gv_ref, state_ref, gk_buf, gv_buf)
        leave(part, 1, (gk_buf, gv_buf))
    for copy in copies:
        copy.wait()


def hbm(shape, dtype):
    return jax.ShapeDtypeStruct(shape, dtype)


def call(body, arrays, outs, flops, scratch=(), raw_in=False, partial=()):
    if raw_in:
        arrays = [pltpu.with_memory_space_constraint(a, pltpu.HBM) for a in arrays]
    vmem, anywhere = pl.BlockSpec(memory_space=pltpu.VMEM), pl.BlockSpec(memory_space=pl.ANY)
    operands = [*arrays, *partial]
    in_specs = [pl.BlockSpec(memory_space=pltpu.HBM) if raw_in else vmem] * len(arrays) + [anywhere] * len(partial)
    whole = [isinstance(out, jax.ShapeDtypeStruct) for out in outs]
    first = whole.index(True) if True in whole else 0
    aliases = {len(arrays) + i: first + i for i in range(len(partial))}
    size = sum(a.size * a.dtype.itemsize for a in arrays) * 2
    return pl.pallas_call(
        body,
        out_shape=outs,
        in_specs=in_specs,
        out_specs=[anywhere if w else vmem for w in whole],
        scratch_shapes=list(scratch),
        input_output_aliases=aliases,
        compiler_params=pltpu.CompilerParams(vmem_limit_bytes=8 * 1024 * 1024),
        cost_estimate=pl.CostEstimate(flops=flops, bytes_accessed=size, transcendentals=0),
    )(*operands)


def swap(value, axes, mask):
    pairs = [(i, i ^ mask) for i in range(lax.axis_size(axes))]
    return lax.ppermute(value, axes, pairs)


def gated(value, bits, level, wanted):
    return jnp.where(bits[level, :1][None] == wanted, value, 0.0)


def before(own, others, target, bits, reverse):
    total = None
    for mask, state in ((0, own), *others.items()):
        if mask != target:
            step = (mask ^ target).bit_length() - 1
            wanted = 1.0 - ((target >> step) & 1)
            term = gated(state, bits, step + 1, 1.0 - wanted if reverse else wanted)
            total = term if total is None else total + term
    return total


def scan_states(plan, sends, keeps, bits, reverse, asides):
    chips = ("seq", "head")
    upper, lower = (0.0, 1.0) if reverse else (1.0, 0.0)
    given = {}

    def beside(name, value, axes, mask):
        if name not in asides:
            return swap(value, axes, mask)
        work, operands = asides[name]
        value, operands = lax.optimization_barrier((value, operands))
        got, given[name] = lax.optimization_barrier((swap(value, axes, mask), work(operands)))
        return got

    share = plan.groups // 2
    members = [range(share), range(share, plan.groups)]
    own, near_got, pair = {}, {}, {}
    for part, (send, keep) in enumerate(zip(sends, keeps)):
        got = swap(send, "sub", 1)
        for number, group in enumerate(members[part]):
            rows = slice(number * plan.kept, (number + 1) * plan.kept)
            own[group], near_got[group] = keep[rows], got[rows].astype(F32)
            pair[group] = own[group] + near_got[group]
    order = [group for part in members for group in part if group]
    others = {}
    for group in order:
        name = "share" if group == order[-1] else ""
        got = beside(name, pair[group].astype(BF), chips, plan.mask(group))
        others[plan.mask(group)] = got.astype(F32)
    total = pair[0]
    for state in others.values():
        total = total + state
    carried = jnp.zeros_like(total)
    for level in range(plan.steps, bits_in(chips)):
        name = "total" if level == bits_in(chips) - 1 else ""
        got = beside(name, total.astype(BF), chips, 1 << level).astype(F32)
        carried = carried + gated(got, bits, level + 1, upper)
        total = total + got
    sums = {0: carried + before(pair[0], others, 0, bits, reverse)}
    for group in order:
        message = carried + before(pair[0], others, plan.mask(group), bits, reverse)
        sums[group] = swap(message.astype(BF), chips, plan.mask(group)).astype(F32)
    near, far, message = [None, None], [None, None], None
    for part in BACK:
        if message is not None:
            for group in members[part]:
                sums[group], message = lax.optimization_barrier((sums[group], message))
            if not reverse:
                far[1 - part] = swap(message, "sub", 1)
            first = message
        message = [sums[group] + gated(own[group], bits, 0, lower) for group in members[part]]
        known = [sums[group] + gated(near_got[group], bits, 0, upper) for group in members[part]]
        message = jnp.concatenate(message).astype(BF)
        near[part] = jnp.concatenate(known).astype(BF)
    if reverse:
        both = swap(jnp.concatenate([message, first]), "sub", 1)
        return near, [both], given
    far[BACK[1]] = swap(message, "sub", 1)
    return near, far, given


def on_device(query, key, value, cot):
    rows, width = query.shape
    plan = Plan(width // HEAD_DIM)
    levels = bits_in(AXES)
    part_state = (plan.part, HEAD_DIM, HEAD_DIM)
    half_state = (plan.half, HEAD_DIM, HEAD_DIM)
    unit = 2 * BLOCK * HEAD_DIM * HEAD_DIM * plan.half
    vm, dma = pltpu.VMEM, pltpu.SemaphoreType.DMA
    whole = hbm((rows, width), BF)
    buf = vm((2, rows, plan.part * HEAD_DIM), BF)

    *states, bits, key_vm, value_vm = call(
        functools.partial(key_value_body, plan), (key, value),
        [vm(part_state, BF)] * 2 + [vm(part_state, F32)] * 2
        + [vm((levels, 8, HEAD_DIM), F32), vm((rows, width), BF), vm((rows, width), BF)],
        unit * 2, (dma((2, 2)),), raw_in=True,
    )

    def inner_work(far, operands):
        return call(
            functools.partial(inner_body, plan, far * plan.half), operands,
            [vm(half_state, BF), vm(half_state, F32)], 2 * unit,
        )

    near, far, given = scan_states(
        plan, states[:2], states[2:], bits, False,
        {
            "share": (functools.partial(inner_work, 0), (query, key_vm, value_vm, cot)),
            "total": (functools.partial(inner_work, 1), (query, key_vm, value_vm)),
        },
    )
    inner = [given["share"], given["total"]]

    def norm(part, is_far, state):
        return call(
            functools.partial(norm_body, plan, plan.base(part, is_far)),
            (query, cot, inner[is_far][1], state),
            [vm(part_state, BF), vm(part_state, BF), vm(part_state, BF if is_far else F32)], unit,
        )

    normed = [[None, None], [None, None]]
    early, late = BACK
    normed[0][early] = norm(early, 0, near[early])
    far[early], normed[0][early] = lax.optimization_barrier((far[early], normed[0][early]))
    for part in BACK:
        normed[1][part] = norm(part, 1, far[part])
    near[late], normed[1] = lax.optimization_barrier((near[late], normed[1]))
    normed[0][late] = norm(late, 0, near[late])
    partials = ()

    def local_grads(is_far, operands):
        nonlocal partials
        out = call(
            functools.partial(local_grads_body, plan, is_far), operands,
            [vm(half_state, F32), vm(half_state, F32), whole, whole],
            5 * unit, (buf, buf, dma((2, 2))), partial=partials,
        )
        partials = out[2:]
        return out[:2]

    def operands(is_far, found):
        parts = [a for part in range(2) for a in (*normed[is_far][part][:2], found[part])]
        return (query, key_vm, value_vm, inner[is_far][0], *parts)

    near, far, given = scan_states(
        plan, [n[2] for n in normed[1]], [n[2] for n in normed[0]], bits, True,
        {
            "share": (functools.partial(local_grads, 0), operands(0, near)),
            "total": (functools.partial(local_grads, 1), operands(1, far)),
        },
    )
    grads = [given["share"], given["total"]]
    normed_out, grad_q = partials
    near_grads = call(
        functools.partial(near_grads_body, plan), (key_vm, value_vm, *grads[0], *near),
        [buf, buf], 2 * unit,
    )
    far, near_grads = lax.optimization_barrier((far, near_grads))
    grad_k, grad_v = call(
        functools.partial(far_grads_body, plan), (key_vm, value_vm, *grads[1], *far, *near_grads),
        [whole, whole], 2 * unit, (buf, buf, dma((2, 2, 2))),
    )
    return normed_out, grad_q, grad_k, grad_v


def solution(mesh):
    placed = P(("group", "seq", "head", "sub"), None)
    return jax.shard_map(
        on_device,
        mesh=mesh,
        in_specs=(placed,) * 4,
        out_specs=(placed,) * 4,
        check_vma=False,
    )
```

```python
import functools

import jax
import jax.numpy as jnp
from jax import lax
from jax.experimental import pallas as pl
from jax.experimental.pallas import tpu as pltpu
from jax.sharding import PartitionSpec as P

HEAD_DIM = 128
BLOCK = 128
EPSILON = 1e-05
BF = jnp.bfloat16
F32 = jnp.float32
NN = (((1,), (0,)), ((), ()))
NT = (((1,), (1,)), ((), ()))
TN = (((0,), (0,)), ((), ()))
AXES = ("seq", "head", "sub")
BACK = (1, 0)


def dot(left, right, form):
    return lax.dot_general(left, right, form, preferred_element_type=F32)


def causal_mask():
    rows = lax.broadcasted_iota(jnp.int32, (BLOCK, BLOCK), 0)
    cols = lax.broadcasted_iota(jnp.int32, (BLOCK, BLOCK), 1)
    return rows >= cols


def place_bit(level):
    place = lax.axis_index(AXES).astype(jnp.int32)
    return lax.bitwise_and(lax.shift_right_logical(place, jnp.int32(level)), jnp.int32(1))


def bits_in(axis):
    return lax.axis_size(axis).bit_length() - 1


class Plan:
    def __init__(self, heads):
        self.heads, self.half = heads, heads // 2
        self.steps = bits_in("head") + (bits_in("seq") > 0)
        self.groups = 1 << self.steps
        self.kept = self.half // self.groups
        self.part = self.half // 2

    def head(self, slot, levels):
        head = jnp.int32(slot)
        for level in levels:
            head = lax.bitwise_xor(head, place_bit(level) * (self.heads >> (level + 1)))
        return head

    def columns(self, slot):
        head = self.head(slot, range(self.steps + 1))
        return pl.ds(pl.multiple_of(head * HEAD_DIM, HEAD_DIM), HEAD_DIM)

    def block(self, part, far):
        head = self.head(self.base(part, far), range(2))
        return pl.ds(pl.multiple_of(head * HEAD_DIM, HEAD_DIM), self.part * HEAD_DIM)

    def inside(self, number):
        head = self.head(number, range(2, self.steps + 1))
        return pl.ds(pl.multiple_of(head * HEAD_DIM, HEAD_DIM), HEAD_DIM)

    def mask(self, group):
        return sum(((group >> (self.steps - 1 - j)) & 1) << j for j in range(self.steps))

    def base(self, part, far):
        return far * self.half + part * self.part

    def side(self, far):
        half = lax.bitwise_xor(jnp.int32(far), place_bit(0)) * (self.half * HEAD_DIM)
        return pl.ds(pl.multiple_of(half, HEAD_DIM), self.half * HEAD_DIM)


def key_value_body(plan, k_ref, v_ref, *rest):
    *parts, bits_ref, k_out, v_out, sems = rest
    copies = {}
    for far in (1, 0):
        at = plan.side(far)
        copies[far] = [
            pltpu.make_async_copy(k_ref.at[:, at], k_out.at[:, at], sems.at[0, far]),
            pltpu.make_async_copy(v_ref.at[:, at], v_out.at[:, at], sems.at[1, far]),
        ]
        for copy in copies[far]:
            copy.start()
    for level in range(bits_ref.shape[0]):
        bits_ref[level] = jnp.full(bits_ref.shape[1:], place_bit(level).astype(F32), F32)
    for far in (1, 0):
        for copy in copies[far]:
            copy.wait()
        for part in (0, 1):
            out_ref = parts[2 * (1 - far) + part]
            for number in range(plan.part):
                at = plan.columns(plan.base(part, far) + number)
                out_ref[number] = dot(k_out[:, at], v_out[:, at], TN).astype(out_ref.dtype)


def inner_body(plan, base, q_ref, k_ref, v_ref, *rest):
    *_, probs_ref, inner_ref = rest
    mask = causal_mask()
    for number in range(plan.half):
        at = plan.columns(base + number)
        probs = jnp.where(mask, dot(q_ref[:, at], k_ref[:, at], NT), 0.0).astype(BF)
        probs_ref[number] = probs
        inner_ref[number] = dot(probs, v_ref[:, at], NN)


def norm_body(plan, base, q_ref, g_ref, inner_ref, state_ref, normed_ref, raw_ref, grad_ref):
    for number in range(plan.part):
        at = plan.columns(base + number)
        query = q_ref[:, at]
        unnormed = inner_ref[base % plan.half + number] + dot(query, state_ref[number], NN)
        inv = lax.rsqrt(jnp.mean(unnormed * unnormed, axis=-1, keepdims=True) + EPSILON)
        normed = unnormed * inv
        normed_ref[number] = normed.astype(BF)
        cot = g_ref[:, at].astype(F32)
        raw = (cot - normed * jnp.mean(cot * normed, axis=-1, keepdims=True)) * inv
        raw = raw.astype(BF)
        raw_ref[number] = raw
        grad_ref[number] = dot(query, raw, TN).astype(grad_ref.dtype)


def local_grads_body(plan, far, q_ref, k_ref, v_ref, probs_ref, *rest):
    found, rest = (rest[:3], rest[3:6]), rest[6:]
    *_, gk_ref, gv_ref, normed_out, gq_out, normed_buf, gq_buf, sems = rest
    mask = causal_mask()
    copies = []
    for part, (normed_ref, raw_ref, state_ref) in enumerate(found):
        for number in range(plan.part):
            normed_buf[part, :, plan.inside(number)] = normed_ref[number]
        to = plan.block(part, far)
        copies.append(pltpu.make_async_copy(normed_buf.at[part], normed_out.at[:, to], sems.at[0, part]))
        copies[-1].start()
    for part, (normed_ref, raw_ref, state_ref) in enumerate(found):
        for number in range(plan.part):
            slot = part * plan.part + number
            at = plan.columns(far * plan.half + slot)
            raw, state = raw_ref[number], state_ref[number]
            grad_probs = jnp.where(mask, dot(raw, v_ref[:, at], NT), 0.0).astype(BF)
            grad_query = dot(grad_probs, k_ref[:, at], NN) + dot(raw, state, NT)
            gq_buf[part, :, plan.inside(number)] = grad_query.astype(BF)
            gk_ref[slot] = dot(grad_probs, q_ref[:, at], TN)
            gv_ref[slot] = dot(probs_ref[slot], raw, TN)
        to = plan.block(part, far)
        copies.append(pltpu.make_async_copy(gq_buf.at[part], gq_out.at[:, to], sems.at[1, part]))
        copies[-1].start()
    for copy in copies:
        copy.wait()


def last_grads(plan, part, far, k_ref, v_ref, gk_ref, gv_ref, state_ref, gk_to, gv_to):
    for number in range(plan.part):
        slot = part * plan.part + number
        at, to = plan.columns(far * plan.half + slot), plan.inside(number)
        state = state_ref[number]
        gk_to[part, :, to] = (gk_ref[slot] + dot(v_ref[:, at], state, NT)).astype(BF)
        gv_to[part, :, to] = (gv_ref[slot] + dot(k_ref[:, at], state, NN)).astype(BF)


def near_grads_body(plan, k_ref, v_ref, gk_ref, gv_ref, *rest):
    *states, gk_out, gv_out = rest
    for part, state_ref in enumerate(states):
        last_grads(plan, part, 0, k_ref, v_ref, gk_ref, gv_ref, state_ref, gk_out, gv_out)


def far_grads_body(plan, k_ref, v_ref, gk_ref, gv_ref, *rest):
    *states, gk_near, gv_near, gk_out, gv_out, gk_buf, gv_buf, sems = rest
    copies = []

    def leave(part, far, pair):
        to = plan.block(part, far)
        for number, (ref, out) in enumerate(zip(pair, (gk_out, gv_out))):
            sem = sems.at[number, far, part]
            copies.append(pltpu.make_async_copy(ref.at[part], out.at[:, to], sem))
            copies[-1].start()

    for part in range(2):
        leave(part, 0, (gk_near, gv_near))
    for part in range(2):
        state_ref = states[0].at[pl.ds(part * plan.part, plan.part)]
        last_grads(plan, part, 1, k_ref, v_ref, gk_ref, gv_ref, state_ref, gk_buf, gv_buf)
        leave(part, 1, (gk_buf, gv_buf))
    for copy in copies:
        copy.wait()


def hbm(shape, dtype):
    return jax.ShapeDtypeStruct(shape, dtype)


def call(body, arrays, outs, flops, scratch=(), raw_in=False, partial=()):
    if raw_in:
        arrays = [pltpu.with_memory_space_constraint(a, pltpu.HBM) for a in arrays]
    vmem, anywhere = pl.BlockSpec(memory_space=pltpu.VMEM), pl.BlockSpec(memory_space=pl.ANY)
    operands = [*arrays, *partial]
    in_specs = [pl.BlockSpec(memory_space=pltpu.HBM) if raw_in else vmem] * len(arrays) + [anywhere] * len(partial)
    whole = [isinstance(out, jax.ShapeDtypeStruct) for out in outs]
    first = whole.index(True) if True in whole else 0
    aliases = {len(arrays) + i: first + i for i in range(len(partial))}
    size = sum(a.size * a.dtype.itemsize for a in arrays) * 2
    return pl.pallas_call(
        body,
        out_shape=outs,
        in_specs=in_specs,
        out_specs=[anywhere if w else vmem for w in whole],
        scratch_shapes=list(scratch),
        input_output_aliases=aliases,
        compiler_params=pltpu.CompilerParams(vmem_limit_bytes=8 * 1024 * 1024),
        cost_estimate=pl.CostEstimate(flops=flops, bytes_accessed=size, transcendentals=0),
    )(*operands)


def swap(value, axes, mask):
    pairs = [(i, i ^ mask) for i in range(lax.axis_size(axes))]
    return lax.ppermute(value, axes, pairs)


def gated(value, bits, level, wanted):
    return jnp.where(bits[level, :1][None] == wanted, value, 0.0)


def before(own, others, target, bits, reverse):
    total = None
    for mask, state in ((0, own), *others.items()):
        if mask != target:
            step = (mask ^ target).bit_length() - 1
            wanted = 1.0 - ((target >> step) & 1)
            term = gated(state, bits, step + 1, 1.0 - wanted if reverse else wanted)
            total = term if total is None else total + term
    return total


def scan_states(plan, sends, keeps, bits, reverse, asides):
    chips = ("seq", "head")
    upper, lower = (0.0, 1.0) if reverse else (1.0, 0.0)
    given = {}

    def beside(name, value, axes, mask):
        if name not in asides:
            return swap(value, axes, mask)
        work, operands = asides[name]
        value, operands = lax.optimization_barrier((value, operands))
        got, given[name] = lax.optimization_barrier((swap(value, axes, mask), work(operands)))
        return got

    share = plan.groups // 2
    members = [range(share), range(share, plan.groups)]
    own, near_got, pair = {}, {}, {}
    for part, (send, keep) in enumerate(zip(sends, keeps)):
        got = swap(send, "sub", 1)
        for number, group in enumerate(members[part]):
            rows = slice(number * plan.kept, (number + 1) * plan.kept)
            own[group], near_got[group] = keep[rows], got[rows].astype(F32)
            pair[group] = own[group] + near_got[group]
    order = [group for part in members for group in part if group]
    others = {}
    for group in order:
        name = "share" if group == order[-1] else ""
        got = beside(name, pair[group].astype(BF), chips, plan.mask(group))
        others[plan.mask(group)] = got.astype(F32)
    total = pair[0]
    for state in others.values():
        total = total + state
    carried = jnp.zeros_like(total)
    for level in range(plan.steps, bits_in(chips)):
        name = "total" if level == bits_in(chips) - 1 else ""
        got = beside(name, total.astype(BF), chips, 1 << level).astype(F32)
        carried = carried + gated(got, bits, level + 1, upper)
        total = total + got
    sums = {0: carried + before(pair[0], others, 0, bits, reverse)}
    for group in order:
        message = carried + before(pair[0], others, plan.mask(group), bits, reverse)
        sums[group] = swap(message.astype(BF), chips, plan.mask(group)).astype(F32)
    near, far, message = [None, None], [None, None], None
    for part in BACK:
        if message is not None:
            for group in members[part]:
                sums[group], message = lax.optimization_barrier((sums[group], message))
            if not reverse:
                far[1 - part] = swap(message, "sub", 1)
            first = message
        message = [sums[group] + gated(own[group], bits, 0, lower) for group in members[part]]
        known = [sums[group] + gated(near_got[group], bits, 0, upper) for group in members[part]]
        message = jnp.concatenate(message).astype(BF)
        near[part] = jnp.concatenate(known).astype(BF)
    if reverse:
        both = swap(jnp.concatenate([message, first]), "sub", 1)
        return near, [both], given
    far[BACK[1]] = swap(message, "sub", 1)
    return near, far, given


def on_device(query, key, value, cot):
    rows, width = query.shape
    plan = Plan(width // HEAD_DIM)
    levels = bits_in(AXES)
    part_state = (plan.part, HEAD_DIM, HEAD_DIM)
    half_state = (plan.half, HEAD_DIM, HEAD_DIM)
    unit = 2 * BLOCK * HEAD_DIM * HEAD_DIM * plan.half
    vm, dma = pltpu.VMEM, pltpu.SemaphoreType.DMA
    whole = hbm((rows, width), BF)
    buf = vm((2, rows, plan.part * HEAD_DIM), BF)

    *states, bits, key_vm, value_vm = call(
        functools.partial(key_value_body, plan), (key, value),
        [vm(part_state, BF)] * 2 + [vm(part_state, F32)] * 2
        + [vm((levels, 8, HEAD_DIM), F32), vm((rows, width), BF), vm((rows, width), BF)],
        unit * 2, (dma((2, 2)),), raw_in=True,
    )

    def inner_work(far, operands):
        return call(
            functools.partial(inner_body, plan, far * plan.half), operands,
            [vm(half_state, BF), vm(half_state, F32)], 2 * unit,
        )

    near, far, given = scan_states(
        plan, states[:2], states[2:], bits, False,
        {
            "share": (functools.partial(inner_work, 0), (query, key_vm, value_vm, cot)),
            "total": (functools.partial(inner_work, 1), (query, key_vm, value_vm)),
        },
    )
    inner = [given["share"], given["total"]]

    def norm(part, is_far, state):
        return call(
            functools.partial(norm_body, plan, plan.base(part, is_far)),
            (query, cot, inner[is_far][1], state),
            [vm(part_state, BF), vm(part_state, BF), vm(part_state, BF if is_far else F32)], unit,
        )

    normed = [[None, None], [None, None]]
    early, late = BACK
    normed[0][early] = norm(early, 0, near[early])
    far, normed[0][early] = lax.optimization_barrier((far, normed[0][early]))
    for part in BACK:
        normed[1][part] = norm(part, 1, far[part])
        if part == early:
            far[late], normed[1][part] = lax.optimization_barrier((far[late], normed[1][part]))
    near[late], normed[1] = lax.optimization_barrier((near[late], normed[1]))
    normed[0][late] = norm(late, 0, near[late])
    partials = ()

    def local_grads(is_far, operands):
        nonlocal partials
        out = call(
            functools.partial(local_grads_body, plan, is_far), operands,
            [vm(half_state, F32), vm(half_state, F32), whole, whole],
            5 * unit, (buf, buf, dma((2, 2))), partial=partials,
        )
        partials = out[2:]
        return out[:2]

    def operands(is_far, found):
        parts = [a for part in range(2) for a in (*normed[is_far][part][:2], found[part])]
        return (query, key_vm, value_vm, inner[is_far][0], *parts)

    near, far, given = scan_states(
        plan, [n[2] for n in normed[1]], [n[2] for n in normed[0]], bits, True,
        {
            "share": (functools.partial(local_grads, 0), operands(0, near)),
            "total": (functools.partial(local_grads, 1), operands(1, far)),
        },
    )
    grads = [given["share"], given["total"]]
    normed_out, grad_q = partials
    near_grads = call(
        functools.partial(near_grads_body, plan), (key_vm, value_vm, *grads[0], *near),
        [buf, buf], 2 * unit,
    )
    far, near_grads = lax.optimization_barrier((far, near_grads))
    grad_k, grad_v = call(
        functools.partial(far_grads_body, plan), (key_vm, value_vm, *grads[1], *far, *near_grads),
        [whole, whole], 2 * unit, (buf, buf, dma((2, 2, 2))),
    )
    return normed_out, grad_q, grad_k, grad_v


def solution(mesh):
    placed = P(("group", "seq", "head", "sub"), None)
    return jax.shard_map(
        on_device,
        mesh=mesh,
        in_specs=(placed,) * 4,
        out_specs=(placed,) * 4,
        check_vma=False,
    )
```
